32 devices in a mesh: dp: 8 (over z, y), expert: 4 (over x, core).
Axes of the slice: x: 2, y: 2, z: 4, core: 2. Of those that a mesh axis runs over, the one named last changes fastest.
Arguments:
- tokens: bfloat16 [1024, 3072], P('expert'), may hold values from -6 to 6
- cotangent: bfloat16 [1024, 3072], P('expert'), may hold values from -6 to 6
- routes: int32 [1024, 2], P('expert'), may hold values from 0 to 3, all different within a row; in each aligned block of 256 rows (0 to 255, 256 to 511, ...) at most 128 rows name the same one
- gate_values: bfloat16 [1024, 2], P('expert'), may hold values from 0.049804688 to 0.94921875
- gate_weight: bfloat16 [4, 3072, 8192], P('expert', None, 'dp'), may hold values from -0.109375 to 0.109375
- up_weight: bfloat16 [4, 3072, 8192], P('expert', None, 'dp'), may hold values from -0.109375 to 0.109375
- down_weight: bfloat16 [4, 3072, 8192], P('expert', None, 'dp'), may hold values from -0.0625 to 0.0625
Outputs:
- clipped: bfloat16 [4, 3, 3072, 8192], P('expert', None, 'dp')
- d_tokens: bfloat16 [3072, 1024], P('dp', 'expert')
The draws below stay inside these ranges and needn't reach their ends.
Inputs may be any that keep to these rules, and one draw needn't show every extreme that they name: `routes`: each row names two different experts. Within the 256 rows of one device along expert (aligned blocks), no expert is named by more than 128 rows.
All inputs are finite; a program needn't handle non-finite values.
Results may differ from the reference program's by a relative error of at most 0.0064.
Values may be sent and summed in bfloat16 or wider, within the bound.
No kernel may reach another device: no remote copies, remote signals or barrier semaphores. Data moves between devices by JAX's collectives and lax.ppermute only.
A program may use at most 128 MiB of HBM per device.

```python
import math
import jax
import jax.numpy as jnp
import numpy as np
from jax import lax

D = 3072
FF = 8192
CAP = 128
TOK_DEV = 256
EXPERTS = 4
TOKENS = 1024
N_EXPERT = 4


def level_of(rng, dims, shards, low, high):
    def one(dim, shards_of):
        draws = jax.random.uniform(jax.random.fold_in(jax.random.fold_in(rng, 6), dim), (shards_of,), jnp.float32, low / len(shards), high / len(shards))
        return jnp.repeat(jnp.exp(draws), dims[dim] // shards_of).reshape((-1,) + (1,) * (len(dims) - dim - 1))

    factor_of = one(*shards[0])
    for cut in shards[1:]:
        factor_of = factor_of * one(*cut)
    return factor_of


def shared_out(key, own, number, rows, amount, top, reach, skew):
    ranking = jax.random.permutation(key, amount)
    crowded, ordinary = load_shares(amount, rows * top, reach, skew, True), load_shares(amount, rows * top, reach, skew, False)
    places = jnp.arange(amount)

    def named(tallies, turn):
        used = int((tallies > 0).sum())
        fixed = max(1, used // 4)
        shifted = fixed + (places - fixed + turn * (used - fixed)) % max(1, amount - fixed)
        return jnp.zeros((amount,), jnp.int32).at[ranking[jnp.where(places < fixed, places, shifted)]].set(jnp.asarray(tallies, jnp.int32))

    tallies = jnp.where(number % 4 == 0, named(crowded, number // 4), named(ordinary, number - number // 4 - 1))
    mixed = jax.random.permutation(jax.random.fold_in(own, 3), amount)
    giver, receiver = mixed[0:amount // 2 * 2:2], mixed[1:amount // 2 * 2:2]
    margin = jnp.minimum(tallies[giver] - 1, reach - tallies[receiver]) // 2
    margin = jnp.where((giver == ranking[0]) | (receiver == ranking[0]) | (tallies[receiver] == 0), 0, jnp.maximum(margin, 0))
    shifted = jax.random.randint(jax.random.fold_in(own, 4), (amount // 2,), 0, 1 << 20) % (margin + 1)
    tallies = tallies.at[giver].add(-shifted).at[receiver].add(shifted)
    members = jnp.searchsorted(jnp.cumsum(tallies), jnp.arange(rows * top), side="right").astype(jnp.int32)
    grid = members.reshape(top, rows).T
    grid = grid[jax.random.permutation(jax.random.fold_in(own, 1), rows)]
    turn = jax.random.randint(jax.random.fold_in(own, 2), (rows, 1), 0, top)
    return jnp.take_along_axis(grid, (jnp.arange(top)[None, :] + turn) % top, axis=1)


def load_shares(number_of, total, bound, lean, full):
    portions = [(1 << 20) // math.isqrt(standing ** lean) + 1 for standing in range(1, number_of + 1)]
    largest = bound if full else min(bound, max(-(-total // number_of), total * portions[0] // sum(portions)))
    least = 1 if total - largest >= number_of - 1 else 0
    given, spare = [largest] + [least] * (number_of - 1), total - largest - least * (number_of - 1)
    while spare > 0:
        candidates = [i for i in range(1, number_of) if given[i] < largest] or [i for i in range(1, number_of) if given[i] < bound]
        whole, remaining = sum([portions[i] for i in candidates]), spare
        for i in candidates:
            more = min(bound - given[i], max(1, remaining * portions[i] // whole), spare)
            given[i] = given[i] + more
            spare = spare - more
    return np.array(given)


def normal_values(rng, dims, spread, limit, split=(), kind=jnp.bfloat16):
    gain = level_of(rng, dims, split, -0.22, 0.18) if split else 1.0
    entries = jax.random.normal(rng, dims, jnp.float32) * spread * gain
    return jnp.minimum(jnp.maximum(entries, -limit), limit).astype(kind)


def setup_inputs(seed: int = 0) -> dict:
    key_list = jax.random.split(jax.random.key(seed), 8)
    tokens = normal_values(key_list[0], (TOKENS, D), 1.0, 6.0, ((0, 4),))
    cotangent = normal_values(key_list[1], (TOKENS, D), 1.0, 6.0, ((0, 4),))
    routes_keys = jax.random.split(jax.random.fold_in(key_list[2], 1), TOKENS // TOK_DEV)
    routes_turns = jax.random.permutation(jax.random.fold_in(key_list[2], 3), TOKENS // TOK_DEV)
    routes = jax.vmap(lambda own, number: shared_out(jax.random.fold_in(key_list[2], 2), own, number, TOK_DEV, EXPERTS, 2, CAP, 2))(routes_keys, routes_turns).reshape((TOKENS, 2))
    gate_values = jnp.clip(0.049804688 + 0.89941406 * jax.random.uniform(key_list[3], (TOKENS, 2), jnp.float32) ** level_of(key_list[3], (TOKENS, 2), ((0, 4),), -0.2, 0.2), 0.049804688, 0.94921875).astype(jnp.bfloat16)
    gate_weight = normal_values(key_list[4], (EXPERTS, D, FF), D ** -0.5, 0.109375, ((0, 4), (2, 8)))
    up_weight = normal_values(key_list[5], (EXPERTS, D, FF), D ** -0.5, 0.109375, ((0, 4), (2, 8)))
    down_weight = normal_values(key_list[6], (EXPERTS, D, FF), FF ** -0.5, 0.0625, ((0, 4), (2, 8)))
    return dict(tokens=tokens, cotangent=cotangent, routes=routes, gate_values=gate_values, gate_weight=gate_weight, up_weight=up_weight, down_weight=down_weight)


CLIP_RMS = 0.2

def slots_of(route_block, experts):
    flat_routes = route_block.reshape(-1).astype(jnp.int32)
    onehot = (flat_routes[:, None] == jnp.arange(experts, dtype=jnp.int32)[None, :]).astype(jnp.int32)
    before = jnp.cumsum(onehot, axis=0) - onehot
    position = lax.optimization_barrier(jnp.sum(before * onehot, axis=1))
    counts = lax.optimization_barrier(jnp.sum(onehot, axis=0))
    return ((flat_routes * CAP + position).astype(jnp.int32), counts)

def fill_rows(token_block, cot_block, gate_block, slot_index, counts, experts):
    routed = slot_index.shape[0]
    row_of_slot = jnp.zeros((experts * CAP,), jnp.int32).at[slot_index].set(jnp.arange(routed, dtype=jnp.int32))
    live_slot = (jnp.arange(CAP, dtype=jnp.int32)[None, :] < counts[:, None]).reshape(-1)
    token_of_slot = row_of_slot // 2
    input_rows = jnp.where(live_slot[:, None], token_block[token_of_slot], jnp.zeros((), token_block.dtype))
    scaled = gate_block.reshape(-1)[row_of_slot].astype(jnp.float32)[:, None] * cot_block[token_of_slot].astype(jnp.float32)
    weighted_rows = jnp.where(live_slot[:, None], scaled, jnp.zeros((), scaled.dtype)).astype(jnp.bfloat16)
    model_width = token_block.shape[1]
    return (input_rows.reshape(experts, CAP, model_width), weighted_rows.reshape(experts, CAP, model_width))

def expert_pass(input_rows, weighted_rows, gate_matrix, up_matrix, down_matrix):
    pre_gate = jnp.dot(input_rows, gate_matrix, preferred_element_type=jnp.float32)
    pre_up = jnp.dot(input_rows, up_matrix, preferred_element_type=jnp.float32)
    sigmoid_gate = jax.nn.sigmoid(pre_gate)
    activated = pre_gate * sigmoid_gate
    hidden = (activated * pre_up).astype(jnp.bfloat16)
    grad_hidden = jnp.dot(weighted_rows, down_matrix, preferred_element_type=jnp.float32)
    grad_gate = (grad_hidden * pre_up * sigmoid_gate * (1.0 + pre_gate * (1.0 - sigmoid_gate))).astype(jnp.bfloat16)
    grad_up = (grad_hidden * activated).astype(jnp.bfloat16)
    stacked = jnp.stack([jnp.dot(input_rows.T, grad_gate, preferred_element_type=jnp.float32), jnp.dot(input_rows.T, grad_up, preferred_element_type=jnp.float32), jnp.dot(weighted_rows.T, hidden, preferred_element_type=jnp.float32)])
    return (stacked, grad_gate, grad_up)

def reference(tokens, cotangent, routes, gate_values, gate_weight, up_weight, down_weight):
    experts = N_EXPERT
    model_width = tokens.shape[1]

    def prepare(inputs):
        token_block, cot_block, route_block, gate_block = inputs
        slot_index, counts = slots_of(route_block, experts)
        input_rows, weighted_rows = fill_rows(token_block, cot_block, gate_block, slot_index, counts, experts)
        return (input_rows, weighted_rows, slot_index)
    input_all, weighted_all, slot_all = lax.map(prepare, (tokens.reshape(experts, TOK_DEV, model_width), cotangent.reshape(experts, TOK_DEV, model_width), routes.reshape(experts, TOK_DEV, 2), gate_values.reshape(experts, TOK_DEV, 2)))
    input_by = jnp.swapaxes(input_all, 0, 1).reshape(experts, experts * CAP, model_width)
    weighted_by = jnp.swapaxes(weighted_all, 0, 1).reshape(experts, experts * CAP, model_width)

    def per_expert(inputs):
        input_rows, weighted_rows, gate_matrix, up_matrix, down_matrix = inputs
        stacked, grad_gate, grad_up = expert_pass(input_rows, weighted_rows, gate_matrix, up_matrix, down_matrix)
        row_grads = jnp.dot(grad_gate, gate_matrix.T, preferred_element_type=jnp.float32) + jnp.dot(grad_up, up_matrix.T, preferred_element_type=jnp.float32)
        return (stacked.astype(jnp.bfloat16), row_grads)
    gradients, row_grads = lax.map(per_expert, (input_by, weighted_by, gate_weight, up_weight, down_weight))
    by_source = jnp.swapaxes(row_grads.reshape(experts, experts, CAP, model_width), 0, 1).reshape(experts, experts * CAP, model_width)

    def combine(inputs):
        source_rows, slot_index = inputs
        gathered = source_rows[slot_index]
        return lax.optimization_barrier(jnp.sum(gathered.reshape(TOK_DEV, 2, model_width), axis=1)).astype(jnp.bfloat16)
    token_grads = lax.map(combine, (by_source, slot_all)).reshape(experts * TOK_DEV, model_width)
    squares = jnp.sum(jnp.square(gradients.astype(jnp.float32)))
    norm = jnp.sqrt(squares)
    clip_limit = CLIP_RMS * math.sqrt(3.0 * experts * model_width * gradients.shape[-1])
    clipped = (gradients.astype(jnp.float32) * (clip_limit / jnp.maximum(norm, clip_limit))).astype(jnp.bfloat16)
    return (clipped, token_grads.T)
```

```python
import functools
import math

import jax
import jax.numpy as jnp
from jax import lax
from jax.experimental import pallas as pl
from jax.experimental.pallas import tpu as pltpu
from jax.sharding import PartitionSpec as P

CAP = 128
CLIP_RMS = 0.2
VMEM = 60 * 1024 * 1024


F32 = jnp.float32
BF16 = jnp.bfloat16


def tile_of(size, largest, unit):
    best = size
    for tile in range(unit, min(size, largest) + 1, unit):
        if size % tile == 0:
            best = tile
    return best


def params(dims=1):
    return pltpu.CompilerParams(
        dimension_semantics=("arbitrary",) * dims, vmem_limit_bytes=VMEM
    )


def dot_nn(left, right):
    return lax.dot_general(left, right, (((1,), (0,)), ((), ())), preferred_element_type=F32)


def dot_nt(left, right):
    return lax.dot_general(left, right, (((1,), (1,)), ((), ())), preferred_element_type=F32)


def dot_tn(left, right):
    return lax.dot_general(left, right, (((0,), (0,)), ((), ())), preferred_element_type=F32)


def stacked(refs):
    tiles = [ref[...] for ref in refs]
    return tiles[0] if len(tiles) == 1 else jnp.concatenate(tiles, axis=0)


def fill_tiles(ids, routes, gates, tokens, cotangent, experts):
    count, width = tokens.shape
    tn = tile_of(width, 768, 128)

    def body(ids_ref, route_ref, gate_ref, tok_ref, cot_ref, *refs):
        x_refs = refs[:experts]
        w_refs = refs[experts : 2 * experts]
        pick_refs = refs[2 * experts : 3 * experts]
        gate_col = refs[3 * experts]

        @pl.when(pl.program_id(0) == 0)
        def _():
            first, second = route_ref[0:1, :], route_ref[1:2, :]
            me = ids_ref[1]
            hits = [
                jnp.logical_or(first == (me ^ r), second == (me ^ r)).astype(F32)
                for r in range(experts)
            ]
            pad = (-experts) % 8
            rows = jnp.concatenate(hits + [jnp.zeros((pad, count), F32)] * (pad > 0), axis=0)
            earlier = (
                lax.broadcasted_iota(jnp.int32, (count, count), 0)
                < lax.broadcasted_iota(jnp.int32, (count, count), 1)
            ).astype(F32)
            before = dot_nn(rows.astype(BF16), earlier.astype(BF16))
            slot = lax.broadcasted_iota(jnp.int32, (CAP, count), 0).astype(F32)
            for r in range(experts):
                match = jnp.logical_and(slot == before[r : r + 1, :], hits[r] > 0.5)
                pick = jnp.where(match, 1.0, 0.0)
                weight = jnp.where(first == (me ^ r), gate_ref[0:1, :], gate_ref[1:2, :])
                gate_col[r * CAP : (r + 1) * CAP, :] = jnp.broadcast_to(
                    jnp.sum(pick * weight, axis=1, keepdims=True), (CAP, 128)
                )
                pick_refs[r][...] = pick.astype(BF16)

        pick = stacked(pick_refs)
        rows = dot_nn(pick, tok_ref[...])
        scaled = dot_nn(pick, cot_ref[...]) * gate_col[:, 0:1]
        for r in range(experts):
            part = slice(r * CAP, (r + 1) * CAP)
            x_refs[r][...] = rows[part].astype(BF16)
            w_refs[r][...] = scaled[part].astype(BF16)

    whole = lambda shape: pl.BlockSpec(shape, lambda j, ids: (0, 0))
    cols = lambda rows: pl.BlockSpec((rows, tn), lambda j, ids: (0, j))
    out = pl.pallas_call(
        body,
        out_shape=[jax.ShapeDtypeStruct((CAP, width), BF16)] * (2 * experts)
        + [jax.ShapeDtypeStruct((CAP, count), BF16)] * experts,
        grid_spec=pltpu.PrefetchScalarGridSpec(
            num_scalar_prefetch=1,
            grid=(width // tn,),
            in_specs=[whole((2, count)), whole((2, count)), cols(count), cols(count)],
            out_specs=[cols(CAP)] * (2 * experts) + [whole((CAP, count))] * experts,
            scratch_shapes=[pltpu.VMEM((experts * CAP, 128), F32)],
        ),
        compiler_params=params(),
        cost_estimate=pl.CostEstimate(
            flops=4 * experts * CAP * count * width,
            bytes_accessed=4 * (count + experts * CAP) * width,
            transcendentals=0,
        ),
        name="fill",
    )(ids, routes, gates, tokens, cotangent)
    return out[:experts], out[experts : 2 * experts], out[2 * experts :]


def expert_units(x_tiles, w_tiles, gate_matrix, up_matrix, down_matrix):
    number = len(x_tiles)
    slots = number * CAP
    width, units = gate_matrix.shape
    tn = tile_of(units, 256, 128)

    def body(*refs):
        x_refs, w_refs = refs[:number], refs[number : 2 * number]
        gate_ref, up_ref, down_ref, hid_ref, gg_ref, gu_ref = refs[2 * number :]
        x, w = stacked(x_refs), stacked(w_refs)
        pre_gate = dot_nn(x, gate_ref[...])
        pre_up = dot_nn(x, up_ref[...])
        grad_hidden = dot_nn(w, down_ref[...])
        sig = jax.nn.sigmoid(pre_gate)
        act = pre_gate * sig
        hid_ref[...] = (act * pre_up).astype(BF16)
        gg_ref[...] = (grad_hidden * pre_up * sig * (1.0 + pre_gate * (1.0 - sig))).astype(BF16)
        gu_ref[...] = (grad_hidden * act).astype(BF16)

    tile = pl.BlockSpec((CAP, width), lambda j: (0, 0), pipeline_mode=pl.Buffered(1))
    mat = pl.BlockSpec((width, tn), lambda j: (0, j))
    return pl.pallas_call(
        body,
        out_shape=[jax.ShapeDtypeStruct((slots, units), BF16)] * 3,
        grid=(units // tn,),
        in_specs=[tile] * (2 * number) + [mat] * 3,
        out_specs=[pl.BlockSpec((slots, tn), lambda j: (0, j))] * 3,
        compiler_params=params(),
        cost_estimate=pl.CostEstimate(
            flops=6 * slots * width * units,
            bytes_accessed=2 * (3 * width * units + 2 * slots * width + 3 * slots * units),
            transcendentals=slots * units,
        ),
        name="units",
    )(*x_tiles, *w_tiles, gate_matrix, up_matrix, down_matrix)


def row_gradients(gg_parts, gu_parts, gate_matrix, up_matrix):
    number = len(gg_parts)
    slots = sum(part.shape[0] for part in gg_parts)
    tiles = slots // CAP
    width, units = gate_matrix.shape
    tn = tile_of(width, 512, 128)

    def body(*refs):
        gg, gu = stacked(refs[:number]), stacked(refs[number : 2 * number])
        gate_ref, up_ref = refs[2 * number : 2 * number + 2]
        outs = refs[2 * number + 2 :]
        grads = (dot_nt(gg, gate_ref[...]) + dot_nt(gu, up_ref[...])).astype(BF16)
        for r in range(tiles):
            outs[r][...] = grads[r * CAP : (r + 1) * CAP]

    held = [pl.BlockSpec(part.shape, lambda j: (0, 0)) for part in gg_parts]
    mat = pl.BlockSpec((tn, units), lambda j: (j, 0))
    return pl.pallas_call(
        body,
        out_shape=[jax.ShapeDtypeStruct((CAP, width), BF16)] * tiles,
        grid=(width // tn,),
        in_specs=held * 2 + [mat] * 2,
        out_specs=[pl.BlockSpec((CAP, tn), lambda j: (0, j))] * tiles,
        compiler_params=params(),
        cost_estimate=pl.CostEstimate(
            flops=4 * slots * width * units,
            bytes_accessed=2 * (2 * width * units + slots * width + 2 * slots * units),
            transcendentals=0,
        ),
        name="rows",
    )(*gg_parts, *gu_parts, gate_matrix, up_matrix)


def square_sum(x_tiles, w_tiles, hid, gg, gu):
    number = len(x_tiles)
    width = x_tiles[0].shape[1]
    units = hid[0].shape[1]
    parts = len(hid)
    tm = tile_of(width, 384, 128)

    def body(*refs):
        x, w = stacked(refs[:number]), stacked(refs[number : 2 * number])
        rest = refs[2 * number :]
        h, a, b = [stacked(rest[k * parts : (k + 1) * parts]) for k in range(3)]
        out_ref, acc = rest[3 * parts :]

        @pl.when(pl.program_id(0) == 0)
        def _():
            acc[...] = jnp.zeros_like(acc)

        total = acc[...]
        for left, right in ((x, a), (x, b), (w, h)):
            grads = dot_tn(left, right).astype(BF16).astype(F32)
            total = total + jnp.sum((grads * grads).reshape(tm // 8, 8, units), axis=0)
        acc[...] = total

        @pl.when(pl.program_id(0) == pl.num_programs(0) - 1)
        def _():
            out_ref[...] = jnp.full((8, 128), jnp.sum(acc[...]), F32)

    tile = pl.BlockSpec((CAP, tm), lambda j: (0, j))
    held = [pl.BlockSpec(part.shape, lambda j: (0, 0)) for part in (*hid, *gg, *gu)]
    slots = number * CAP
    return pl.pallas_call(
        body,
        out_shape=jax.ShapeDtypeStruct((8, 128), F32),
        grid=(width // tm,),
        in_specs=[tile] * (2 * number) + held,
        out_specs=pl.BlockSpec((8, 128), lambda j: (0, 0)),
        scratch_shapes=[pltpu.VMEM((8, units), F32)],
        compiler_params=params(),
        cost_estimate=pl.CostEstimate(
            flops=6 * slots * width * units,
            bytes_accessed=2 * (2 * slots * width + 3 * slots * units),
            transcendentals=0,
        ),
        name="squares",
    )(*x_tiles, *w_tiles, *hid, *gg, *gu)


def clipped_rows(ids, scale, x_own, w_own, hid, gg, gu, out, owner, shards):
    rows, slots = x_own.shape
    units = hid[0].shape[1]
    parts = len(hid)

    def body(ids_ref, scale_ref, x_ref, w_ref, *rest):
        h, a, b = [stacked(rest[k * parts : (k + 1) * parts]) for k in range(3)]
        out_ref = rest[-1]
        factor = scale_ref[0, 0]
        x, w = x_ref[...], w_ref[...]
        for k, (left, right) in enumerate(((x, a), (x, b), (w, h))):
            grads = dot_nn(left, right).astype(BF16).astype(F32)
            out_ref[k] = (grads * factor).astype(BF16)

    held = [pl.BlockSpec(part.shape, lambda j, ids: (0, 0)) for part in (*hid, *gg, *gu)]
    operands = [ids, scale, x_own, w_own, *hid, *gg, *gu]
    specs = [pl.BlockSpec(memory_space=pltpu.SMEM)]
    specs += [pl.BlockSpec((rows, slots), lambda j, ids: (0, 0))] * 2 + held
    aliases = {}
    if out is not None:
        aliases = {len(operands): 0}
        operands.append(out)
        specs.append(pl.BlockSpec(memory_space=pl.ANY))
    return pl.pallas_call(
        body,
        out_shape=jax.ShapeDtypeStruct((3, rows, units * shards), BF16),
        grid_spec=pltpu.PrefetchScalarGridSpec(
            num_scalar_prefetch=1,
            grid=(1,),
            in_specs=specs,
            out_specs=pl.BlockSpec((3, rows, units), lambda j, ids: (0, 0, owner(ids[0]))),
        ),
        input_output_aliases=aliases,
        compiler_params=params(),
        cost_estimate=pl.CostEstimate(
            flops=6 * slots * rows * units,
            bytes_accessed=2 * (2 * slots * rows + 3 * slots * units + 3 * rows * units),
            transcendentals=0,
        ),
        name="clip",
    )(*operands)


def token_sums(tiles, picks):
    number = len(tiles)
    width = tiles[0].shape[1]
    count = picks[0].shape[1]
    tn = tile_of(width, 768, 128)

    def body(*refs):
        rows, pick = stacked(refs[:number]), stacked(refs[number : 2 * number])
        refs[2 * number][...] = dot_tn(rows, pick)

    return pl.pallas_call(
        body,
        out_shape=jax.ShapeDtypeStruct((width, count), F32),
        grid=(width // tn,),
        in_specs=[pl.BlockSpec((CAP, tn), lambda j: (0, j))] * number
        + [pl.BlockSpec((CAP, count), lambda j: (0, 0))] * number,
        out_specs=pl.BlockSpec((tn, count), lambda j: (j, 0)),
        compiler_params=params(),
        cost_estimate=pl.CostEstimate(
            flops=2 * number * CAP * width * count,
            bytes_accessed=2 * number * CAP * width + 4 * width * count,
            transcendentals=0,
        ),
        name="combine",
    )(*tiles, *picks)


def per_device(tokens, cotangent, routes, gate_values, gate_weight, up_weight, down_weight):
    experts = lax.axis_size("expert")
    shards = lax.axis_size("dp")
    width = tokens.shape[1]
    gate_matrix, up_matrix, down_matrix = gate_weight[0], up_weight[0], down_weight[0]
    units = gate_matrix.shape[1]
    half = shards // 2
    ids = jnp.stack([lax.axis_index("dp"), lax.axis_index("expert")]).astype(jnp.int32)

    def swap(value, axis, size, bit):
        return lax.ppermute(value, axis, [(i, i ^ bit) for i in range(size)])

    x_send, w_send, picks = fill_tiles(
        ids, routes.T, gate_values.T.astype(F32), tokens, cotangent, experts
    )
    x_tiles = [x_send[0]] + [swap(x_send[r], "expert", experts, r) for r in range(1, experts)]
    w_tiles = [w_send[0]] + [swap(w_send[r], "expert", experts, r) for r in range(1, experts)]
    near = slice(0, min(2, experts))
    far = slice(min(2, experts), experts)
    groups = [group for group in (near, far) if len(x_tiles[group])]
    values = [
        expert_units(x_tiles[group], w_tiles[group], gate_matrix, up_matrix, down_matrix)
        for group in groups
    ]
    parts = len(values)
    own = [values[p][k] for p in range(parts) for k in range(3)]

    order = [2 * i for i in range(half)] + [2 * i + 1 for i in reversed(range(half))]
    right = [(order[p], order[(p + 1) % shards]) for p in range(shards)]
    left = [(b, a) for a, b in right]

    def owner_at(step):
        def owner(index):
            place = jnp.where(index % 2 == 0, index // 2, shards - 1 - index // 2)
            source = (place + shards - step) % shards
            return jnp.where(source < half, 2 * source, 2 * (shards - 1 - source) + 1)

        return owner

    chunks = {0: own}
    from_left, from_right = list(own), list(own)
    for step in range(1, half):
        from_left = [lax.ppermute(v, "dp", right) for v in from_left]
        from_right = [lax.ppermute(v, "dp", left) for v in from_right]
        chunks[step] = from_left
        chunks[shards - step] = from_right
    chunks[half] = [
        lax.ppermute(from_left[i], "dp", right) if i % 2 == 0 else lax.ppermute(from_right[i], "dp", left)
        for i in range(len(own))
    ]

    split = lambda chunk: [[chunk[3 * p + k] for p in range(parts)] for k in range(3)]
    hid, gg, gu = split(own)
    total = square_sum(x_tiles, w_tiles, hid, gg, gu)
    bit = 1
    while bit < experts:
        total = total + swap(total, "expert", experts, bit)
        bit *= 2
    bit = 1
    while bit < shards:
        total = total + swap(total, "dp", shards, bit)
        bit *= 2
    clip_limit = CLIP_RMS * math.sqrt(3.0 * experts * width * units * shards)
    scale = clip_limit / jnp.maximum(jnp.sqrt(total[0:1, 0:1]), clip_limit)

    sent = row_gradients(gg, gu, gate_matrix, up_matrix)
    back = [sent[0]] + [swap(sent[r], "expert", experts, r) for r in range(1, experts)]
    rows = width // shards
    outer, inner = ids[0] // 2, ids[0] % 2
    partial = token_sums(back, picks).reshape(half, 2, rows, tokens.shape[0])
    send = lax.dynamic_index_in_dim(partial, 1 - inner, 1, keepdims=False).astype(BF16)
    keep = lax.dynamic_index_in_dim(partial, inner, 1, keepdims=False)
    sums = keep + swap(send, "dp", shards, 1).astype(F32)
    d_tokens = lax.dynamic_index_in_dim(sums, outer, 0, keepdims=False)
    for turn in range(1, half):
        part = lax.dynamic_index_in_dim(sums, (outer + turn) % half, 0, keepdims=False).astype(BF16)
        route = [(2 * i + j, 2 * ((i + turn) % half) + j) for i in range(half) for j in range(2)]
        d_tokens = d_tokens + lax.ppermute(part, "dp", route).astype(F32)
    d_tokens = d_tokens.astype(BF16)

    def own_rows(tiles):
        mine = [lax.dynamic_slice_in_dim(tile, ids[0] * rows, rows, 1) for tile in tiles]
        return jnp.concatenate(mine, axis=0).T

    x_own, w_own = own_rows(x_tiles), own_rows(w_tiles)
    out = None
    sequence = [0] + [s for step in range(1, half) for s in (step, shards - step)] + [half]
    for step in sequence:
        hid, gg, gu = split(chunks[step])
        out = clipped_rows(
            ids, scale, x_own, w_own, hid, gg, gu, out, owner_at(step), shards
        )
    return (out[None], d_tokens)


def solution(mesh):
    return jax.shard_map(
        per_device,
        mesh=mesh,
        in_specs=(
            P("expert", None),
            P("expert", None),
            P("expert", None),
            P("expert", None),
            P("expert", None, "dp"),
            P("expert", None, "dp"),
            P("expert", None, "dp"),
        ),
        out_specs=(P("expert", None, "dp", None), P("dp", "expert")),
        check_vma=False,
    )
```

```python
import functools
import math

import jax
import jax.numpy as jnp
from jax import lax
from jax.experimental import pallas as pl
from jax.experimental.pallas import tpu as pltpu
from jax.sharding import PartitionSpec as P


CAP = 128
CLIP_RMS = 0.2
VMEM = 60 * 1024 * 1024


F32 = jnp.float32
BF16 = jnp.bfloat16


def tile_of(size, largest, unit):
    best = size
    for tile in range(unit, min(size, largest) + 1, unit):
        if size % tile == 0:
            best = tile
    return best


def params(dims=1):
    return pltpu.CompilerParams(
        dimension_semantics=("arbitrary",) * dims, vmem_limit_bytes=VMEM
    )


def dot_nn(left, right):
    return lax.dot_general(left, right, (((1,), (0,)), ((), ())), preferred_element_type=F32)


def dot_nt(left, right):
    return lax.dot_general(left, right, (((1,), (1,)), ((), ())), preferred_element_type=F32)


def dot_tn(left, right):
    return lax.dot_general(left, right, (((0,), (0,)), ((), ())), preferred_element_type=F32)


free = pl.BlockSpec(memory_space=pl.ANY)


def planes(refs, plane):
    tiles = [ref[plane] for ref in refs]
    return tiles[0] if len(tiles) == 1 else jnp.concatenate(tiles, axis=0)


def stacked(refs):
    tiles = [ref[...] for ref in refs]
    return tiles[0] if len(tiles) == 1 else jnp.concatenate(tiles, axis=0)


def fill_tiles(ids, routes, gates, tokens, cotangent, experts):
    count, width = tokens.shape
    tn = tile_of(width, 768, 128)

    def body(ids_ref, route_ref, gate_ref, tok_ref, cot_ref, *refs):
        x_refs = refs[:experts]
        w_refs = refs[experts : 2 * experts]
        pick_refs = refs[2 * experts : 3 * experts]
        gate_col = refs[3 * experts]

        @pl.when(pl.program_id(0) == 0)
        def _():
            first, second = route_ref[0:1, :], route_ref[1:2, :]
            me = ids_ref[1]
            hits = [
                jnp.logical_or(first == (me ^ r), second == (me ^ r)).astype(F32)
                for r in range(experts)
            ]
            pad = (-experts) % 8
            rows = jnp.concatenate(hits + [jnp.zeros((pad, count), F32)] * (pad > 0), axis=0)
            earlier = (
                lax.broadcasted_iota(jnp.int32, (count, count), 0)
                < lax.broadcasted_iota(jnp.int32, (count, count), 1)
            ).astype(F32)
            before = dot_nn(rows.astype(BF16), earlier.astype(BF16))
            slot = lax.broadcasted_iota(jnp.int32, (CAP, count), 0).astype(F32)
            for r in range(experts):
                match = jnp.logical_and(slot == before[r : r + 1, :], hits[r] > 0.5)
                pick = jnp.where(match, 1.0, 0.0)
                weight = jnp.where(first == (me ^ r), gate_ref[0:1, :], gate_ref[1:2, :])
                gate_col[r * CAP : (r + 1) * CAP, :] = jnp.broadcast_to(
                    jnp.sum(pick * weight, axis=1, keepdims=True), (CAP, 128)
                )
                pick_refs[r][...] = pick.astype(BF16)

        pick = stacked(pick_refs)
        rows = dot_nn(pick, tok_ref[...])
        scaled = dot_nn(pick, cot_ref[...]) * gate_col[:, 0:1]
        for r in range(experts):
            part = slice(r * CAP, (r + 1) * CAP)
            x_refs[r][...] = rows[part].astype(BF16)
            w_refs[r][...] = scaled[part].astype(BF16)

    whole = lambda shape: pl.BlockSpec(shape, lambda j, ids: (0, 0))
    cols = lambda rows: pl.BlockSpec((rows, tn), lambda j, ids: (0, j))
    out = pl.pallas_call(
        body,
        out_shape=[jax.ShapeDtypeStruct((CAP, width), BF16)] * (2 * experts)
        + [jax.ShapeDtypeStruct((CAP, count), BF16)] * experts,
        grid_spec=pltpu.PrefetchScalarGridSpec(
            num_scalar_prefetch=1,
            grid=(width // tn,),
            in_specs=[whole((2, count)), whole((2, count)), cols(count), cols(count)],
            out_specs=[cols(CAP)] * (2 * experts) + [whole((CAP, count))] * experts,
            scratch_shapes=[pltpu.VMEM((experts * CAP, 128), F32)],
        ),
        compiler_params=params(),
        cost_estimate=pl.CostEstimate(
            flops=4 * experts * CAP * count * width,
            bytes_accessed=4 * (count + experts * CAP) * width,
            transcendentals=0,
        ),
        name="fill",
    )(ids, routes, gates, tokens, cotangent)
    return out[:experts], out[experts : 2 * experts], out[2 * experts :]


def expert_units(x_tiles, w_tiles, gate_matrix, up_matrix, down_matrix, after):
    number = len(x_tiles)
    slots = number * CAP
    width, units = gate_matrix.shape
    tn = tile_of(units, 256, 128)

    def body(*refs):
        x_refs, w_refs = refs[:number], refs[number : 2 * number]
        gate_ref, up_ref, down_ref = refs[2 * number : 2 * number + 3]
        out_ref = refs[-1]
        x, w = stacked(x_refs), stacked(w_refs)
        pre_gate = dot_nn(x, gate_ref[...])
        pre_up = dot_nn(x, up_ref[...])
        grad_hidden = dot_nn(w, down_ref[...])
        sig = jax.nn.sigmoid(pre_gate)
        act = pre_gate * sig
        out_ref[0] = (act * pre_up).astype(BF16)
        out_ref[1] = (grad_hidden * pre_up * sig * (1.0 + pre_gate * (1.0 - sig))).astype(BF16)
        out_ref[2] = (grad_hidden * act).astype(BF16)

    tile = pl.BlockSpec((CAP, width), lambda j: (0, 0), pipeline_mode=pl.Buffered(1))
    mat = pl.BlockSpec((width, tn), lambda j: (0, j))
    return pl.pallas_call(
        body,
        out_shape=jax.ShapeDtypeStruct((3, slots, units), BF16),
        grid=(units // tn,),
        in_specs=[tile] * (2 * number) + [mat] * 3 + [free] * len(after),
        out_specs=pl.BlockSpec((3, slots, tn), lambda j: (0, 0, j)),
        compiler_params=params(),
        cost_estimate=pl.CostEstimate(
            flops=6 * slots * width * units,
            bytes_accessed=2 * (3 * width * units + 2 * slots * width + 3 * slots * units),
            transcendentals=slots * units,
        ),
        name="units",
    )(*x_tiles, *w_tiles, gate_matrix, up_matrix, down_matrix, *after)


def row_gradients(values, gate_matrix, up_matrix):
    slots = values.shape[1]
    tiles = slots // CAP
    width, units = gate_matrix.shape
    tn = tile_of(width, 512, 128)

    def body(value_ref, gate_ref, up_ref, *outs):
        grads = dot_nt(value_ref[1], gate_ref[...]) + dot_nt(value_ref[2], up_ref[...])
        grads = grads.astype(BF16)
        for r in range(tiles):
            outs[r][...] = grads[r * CAP : (r + 1) * CAP]

    mat = pl.BlockSpec((tn, units), lambda j: (j, 0))
    return pl.pallas_call(
        body,
        out_shape=[jax.ShapeDtypeStruct((CAP, width), BF16)] * tiles,
        grid=(width // tn,),
        in_specs=[pl.BlockSpec(values.shape, lambda j: (0, 0, 0))] + [mat] * 2,
        out_specs=[pl.BlockSpec((CAP, tn), lambda j: (0, j))] * tiles,
        compiler_params=params(),
        cost_estimate=pl.CostEstimate(
            flops=4 * slots * width * units,
            bytes_accessed=2 * (2 * width * units + slots * width + 3 * slots * units),
            transcendentals=0,
        ),
        name="rows",
    )(values, gate_matrix, up_matrix)


def square_sum(x_tiles, w_tiles, values):
    number = len(x_tiles)
    width = x_tiles[0].shape[1]
    units = values[0].shape[2]
    parts = len(values)
    tm = tile_of(width, 384, 128)

    def body(*refs):
        x, w = stacked(refs[:number]), stacked(refs[number : 2 * number])
        value_refs = refs[2 * number : 2 * number + parts]
        out_ref, acc = refs[2 * number + parts :]

        @pl.when(pl.program_id(0) == 0)
        def _():
            acc[...] = jnp.zeros_like(acc)

        total = acc[...]
        for k, left in enumerate((w, x, x)):
            grads = dot_tn(left, planes(value_refs, k)).astype(BF16).astype(F32)
            total = total + jnp.sum((grads * grads).reshape(tm // 8, 8, units), axis=0)
        acc[...] = total

        @pl.when(pl.program_id(0) == pl.num_programs(0) - 1)
        def _():
            out_ref[...] = jnp.full((8, 128), jnp.sum(acc[...]), F32)

    tile = pl.BlockSpec((CAP, tm), lambda j: (0, j))
    slots = number * CAP
    return pl.pallas_call(
        body,
        out_shape=jax.ShapeDtypeStruct((8, 128), F32),
        grid=(width // tm,),
        in_specs=[tile] * (2 * number)
        + [pl.BlockSpec(value.shape, lambda j: (0, 0, 0)) for value in values],
        out_specs=pl.BlockSpec((8, 128), lambda j: (0, 0)),
        scratch_shapes=[pltpu.VMEM((8, units), F32)],
        compiler_params=params(),
        cost_estimate=pl.CostEstimate(
            flops=6 * slots * width * units,
            bytes_accessed=2 * (2 * slots * width + 3 * slots * units),
            transcendentals=0,
        ),
        name="squares",
    )(*x_tiles, *w_tiles, *values)


def own_columns(x_own, w_own):
    slots, rows = x_own.shape

    def body(x_ref, w_ref, xt_ref, wt_ref):
        xt_ref[...] = x_ref[...].T
        wt_ref[...] = w_ref[...].T

    return pl.pallas_call(
        body,
        out_shape=[jax.ShapeDtypeStruct((rows, slots), BF16)] * 2,
        compiler_params=pltpu.CompilerParams(vmem_limit_bytes=VMEM),
        name="own",
    )(x_own, w_own)


def clipped_rows(ids, scale, x_own, w_own, values, out, owner, shards):
    rows, slots = x_own.shape
    units = values[0].shape[2]
    parts = len(values)
    tn = tile_of(units, 256, 128)
    steps = units // tn

    def body(ids_ref, scale_ref, x_ref, w_ref, *rest):
        value_refs, out_ref = rest[:parts], rest[-1]
        factor = scale_ref[0, 0]
        x, w = x_ref[...], w_ref[...]
        for k, left in enumerate((w, x, x)):
            grads = dot_nn(left, planes(value_refs, k)).astype(BF16).astype(F32)
            out_ref[(k + 2) % 3] = (grads * factor).astype(BF16)

    operands = [ids, scale, x_own, w_own, *values]
    specs = [pl.BlockSpec(memory_space=pltpu.SMEM)]
    specs += [pl.BlockSpec((rows, slots), lambda j, ids: (0, 0))] * 2
    specs += [pl.BlockSpec((*value.shape[:2], tn), lambda j, ids: (0, 0, j)) for value in values]
    aliases = {}
    if out is not None:
        aliases = {len(operands): 0}
        operands.append(out)
        specs.append(free)
    return pl.pallas_call(
        body,
        out_shape=jax.ShapeDtypeStruct((3, rows, units * shards), BF16),
        grid_spec=pltpu.PrefetchScalarGridSpec(
            num_scalar_prefetch=1,
            grid=(steps,),
            in_specs=specs,
            out_specs=pl.BlockSpec(
                (3, rows, tn), lambda j, ids: (0, 0, owner(ids[0]) * steps + j)
            ),
        ),
        input_output_aliases=aliases,
        compiler_params=params(),
        cost_estimate=pl.CostEstimate(
            flops=6 * slots * rows * units,
            bytes_accessed=2 * (2 * slots * rows + 3 * slots * units + 3 * rows * units),
            transcendentals=0,
        ),
        name="clip",
    )(*operands)


def token_sums(tiles, picks):
    number = len(tiles)
    width = tiles[0].shape[1]
    count = picks[0].shape[1]
    tn = tile_of(width, 768, 128)

    def body(*refs):
        rows, pick = stacked(refs[:number]), stacked(refs[number : 2 * number])
        refs[2 * number][...] = dot_tn(rows, pick)

    return pl.pallas_call(
        body,
        out_shape=jax.ShapeDtypeStruct((width, count), F32),
        grid=(width // tn,),
        in_specs=[pl.BlockSpec((CAP, tn), lambda j: (0, j))] * number
        + [pl.BlockSpec((CAP, count), lambda j: (0, 0))] * number,
        out_specs=pl.BlockSpec((tn, count), lambda j: (j, 0)),
        compiler_params=params(),
        cost_estimate=pl.CostEstimate(
            flops=2 * number * CAP * width * count,
            bytes_accessed=2 * number * CAP * width + 4 * width * count,
            transcendentals=0,
        ),
        name="combine",
    )(*tiles, *picks)


def per_device(tokens, cotangent, routes, gate_values, gate_weight, up_weight, down_weight):
    experts = lax.axis_size("expert")
    shards = lax.axis_size("dp")
    width = tokens.shape[1]
    gate_matrix, up_matrix, down_matrix = gate_weight[0], up_weight[0], down_weight[0]
    units = gate_matrix.shape[1]
    half = shards // 2
    rows = width // shards
    ids = jnp.stack([lax.axis_index("dp"), lax.axis_index("expert")]).astype(jnp.int32)

    def swap(value, axis, size, bit):
        return lax.ppermute(value, axis, [(i, i ^ bit) for i in range(size)])

    x_send, w_send, picks = fill_tiles(
        ids, routes.T, gate_values.T.astype(F32), tokens, cotangent, experts
    )
    x_tiles, w_tiles = list(x_send[:1]), list(w_send[:1])
    for r in range(1, experts):
        x_tiles.append(swap(x_send[r], "expert", experts, r))
        w_tiles.append(swap(w_send[r], "expert", experts, r))
    near = min(2, experts)
    groups = [slice(0, near), slice(near, experts)][: 1 + (experts > near)]
    own = []
    for group in groups:
        own.append(
            expert_units(
                x_tiles[group], w_tiles[group], gate_matrix, up_matrix, down_matrix, own[-1:]
            )
        )

    order = [2 * i for i in range(half)] + [2 * i + 1 for i in reversed(range(half))]
    right = [(order[p], order[(p + 1) % shards]) for p in range(shards)]
    left = [(b, a) for a, b in right]

    def owner_at(step):
        def owner(index):
            place = jnp.where(index % 2 == 0, index // 2, shards - 1 - index // 2)
            source = (place + shards - step) % shards
            return jnp.where(source < half, 2 * source, 2 * (shards - 1 - source) + 1)

        return owner

    def hop(value, way):
        return lax.ppermute(value, "dp", right if way == "r" else left)

    chunks = {0: own}
    from_left, from_right = own, own
    for step in range(1, half):
        from_left = [hop(v, "r") for v in from_left]
        from_right = [hop(v, "l") for v in from_right]
        chunks[step] = from_left
        chunks[shards - step] = from_right
    chunks[half] = [
        hop(from_left[p], "r") if p == 0 else hop(from_right[p], "l")
        for p in range(len(own))
    ]

    total = square_sum(x_tiles, w_tiles, own)
    bit = 1
    while bit < experts:
        total = total + swap(total, "expert", experts, bit)
        bit *= 2
    shares = [total]
    for k in range(1, shards):
        shares.append(swap(total, "dp", shards, k))
    total = functools.reduce(lambda a, b: a + b, shares)
    clip_limit = CLIP_RMS * math.sqrt(3.0 * experts * width * units * shards)
    scale = clip_limit / jnp.maximum(jnp.sqrt(total[0:1, 0:1]), clip_limit)

    sent = []
    for value in own:
        sent += row_gradients(value, gate_matrix, up_matrix)
    back = sent[:1]
    for r in range(1, experts):
        back.append(swap(sent[r], "expert", experts, r))
    outer, inner = ids[0] // 2, ids[0] % 2
    partial = token_sums(back, picks).reshape(half, 2, rows, tokens.shape[0])
    send = lax.dynamic_index_in_dim(partial, 1 - inner, 1, keepdims=False).astype(BF16)
    keep = lax.dynamic_index_in_dim(partial, inner, 1, keepdims=False)
    sums = keep + swap(send, "dp", shards, 1).astype(F32)
    d_tokens = lax.dynamic_index_in_dim(sums, outer, 0, keepdims=False)
    for turn in range(1, half):
        part = lax.dynamic_index_in_dim(sums, (outer + turn) % half, 0, keepdims=False).astype(BF16)
        route = [(2 * i + j, 2 * ((i + turn) % half) + j) for i in range(half) for j in range(2)]
        d_tokens = d_tokens + lax.ppermute(part, "dp", route).astype(F32)
    d_tokens = d_tokens.astype(BF16)

    def own_rows(tiles):
        mine = [lax.dynamic_slice_in_dim(tile, ids[0] * rows, rows, 1) for tile in tiles]
        return jnp.concatenate(mine, axis=0)

    x_own, w_own = own_columns(own_rows(x_tiles), own_rows(w_tiles))
    out = None
    for step in clip_order(shards):
        out = clipped_rows(ids, scale, x_own, w_own, chunks[step], out, owner_at(step), shards)
    return (out[None], d_tokens)


def clip_order(shards):
    half = shards // 2
    order = [0, 1, shards - 1]
    for step in range(2, half):
        order += [shards - step, step]
    return order + [half]


def solution(mesh):
    return jax.shard_map(
        per_device,
        mesh=mesh,
        in_specs=(
            P("expert", None),
            P("expert", None),
            P("expert", None),
            P("expert", None),
            P("expert", None, "dp"),
            P("expert", None, "dp"),
            P("expert", None, "dp"),
        ),
        out_specs=(P("expert", None, "dp", None), P("dp", "expert")),
        check_vma=False,
    )
```

```python
import functools
import math

import jax
import jax.numpy as jnp
from jax import lax
from jax.experimental import pallas as pl
from jax.experimental.pallas import tpu as pltpu
from jax.sharding import PartitionSpec as P


CAP = 128
CLIP_RMS = 0.2
VMEM = 67043328


F32 = jnp.float32
BF16 = jnp.bfloat16


def tile_of(size, largest, unit):
    best = size
    for tile in range(unit, min(size, largest) + 1, unit):
        if size % tile == 0:
            best = tile
    return best


def params(dims=1):
    return pltpu.CompilerParams(
        dimension_semantics=("arbitrary",) * dims, vmem_limit_bytes=VMEM
    )


def dot_nn(left, right):
    return lax.dot_general(left, right, (((1,), (0,)), ((), ())), preferred_element_type=F32)


def dot_nt(left, right):
    return lax.dot_general(left, right, (((1,), (1,)), ((), ())), preferred_element_type=F32)


def dot_tn(left, right):
    return lax.dot_general(left, right, (((0,), (0,)), ((), ())), preferred_element_type=F32)


free = pl.BlockSpec(memory_space=pl.ANY)


def planes(refs, splits, plane):
    tiles, at = [], 0
    for count in splits:
        pieces = [ref[plane] for ref in refs[at : at + count]]
        tiles.append(pieces[0] if count == 1 else jnp.concatenate(pieces, axis=1))
        at += count
    return tiles[0] if len(tiles) == 1 else jnp.concatenate(tiles, axis=0)


def flat(parts):
    return [piece for part in parts for piece in part]


def held(values):
    return [pl.BlockSpec(value.shape, lambda *_: (0, 0, 0)) for value in values]


def stacked(refs):
    tiles = [ref[...] for ref in refs]
    return tiles[0] if len(tiles) == 1 else jnp.concatenate(tiles, axis=0)


def route_tiles(me, route_ref, gate_ref, pick_refs, gate_col, tiles):
    count = route_ref.shape[1]
    first, second = route_ref[0:1, :], route_ref[1:2, :]
    gates = gate_ref[...].astype(F32)
    hits = [jnp.logical_or(first == (me ^ r), second == (me ^ r)).astype(F32) for r in tiles]
    pad = (-len(tiles)) % 8
    rows = jnp.concatenate(hits + [jnp.zeros((pad, count), F32)] * (pad > 0), axis=0)
    earlier = (
        lax.broadcasted_iota(jnp.int32, (count, count), 0)
        < lax.broadcasted_iota(jnp.int32, (count, count), 1)
    ).astype(F32)
    before = dot_nn(rows.astype(BF16), earlier.astype(BF16))
    slot = lax.broadcasted_iota(jnp.int32, (CAP, count), 0).astype(F32)
    for k, r in enumerate(tiles):
        match = jnp.logical_and(slot == before[k : k + 1, :], hits[k] > 0.5)
        pick = jnp.where(match, 1.0, 0.0)
        weight = jnp.where(first == (me ^ r), gates[0:1, :], gates[1:2, :])
        gate_col[k * CAP : (k + 1) * CAP, :] = jnp.broadcast_to(
            jnp.sum(pick * weight, axis=1, keepdims=True), (CAP, 128)
        )
        pick_refs[k][...] = pick.astype(BF16)


def fill_rows(pick_refs, gate_col, tok_ref, cot_ref, x_refs, w_refs):
    pick = stacked(pick_refs)
    rows = dot_nn(pick, tok_ref[...])
    scaled = dot_nn(pick, cot_ref[...]) * gate_col[:, 0:1]
    for k in range(len(x_refs)):
        part = slice(k * CAP, (k + 1) * CAP)
        x_refs[k][...] = rows[part].astype(BF16)
        w_refs[k][...] = scaled[part].astype(BF16)


def fill_tiles(ids, routes, gates, tokens, cotangent, tiles):
    count, width = tokens.shape
    number = len(tiles)
    tn = tile_of(width, 1536, 128)

    def body(ids_ref, route_ref, gate_ref, tok_ref, cot_ref, *refs):
        x_refs, w_refs = refs[:number], refs[number : 2 * number]
        pick_refs, gate_col = refs[2 * number : 3 * number], refs[3 * number]

        @pl.when(pl.program_id(0) == 0)
        def _():
            route_tiles(ids_ref[1], route_ref, gate_ref, pick_refs, gate_col, tiles)

        fill_rows(pick_refs, gate_col, tok_ref, cot_ref, x_refs, w_refs)

    whole = lambda shape: pl.BlockSpec(shape, lambda j, ids: (0, 0))
    cols = lambda rows: pl.BlockSpec((rows, tn), lambda j, ids: (0, j))
    out = pl.pallas_call(
        body,
        out_shape=[jax.ShapeDtypeStruct((CAP, width), BF16)] * (2 * number)
        + [jax.ShapeDtypeStruct((CAP, count), BF16)] * number,
        grid_spec=pltpu.PrefetchScalarGridSpec(
            num_scalar_prefetch=1,
            grid=(width // tn,),
            in_specs=[whole((2, count)), whole((2, count)), cols(count), cols(count)],
            out_specs=[cols(CAP)] * (2 * number) + [whole((CAP, count))] * number,
            scratch_shapes=[pltpu.VMEM((number * CAP, 128), F32)],
        ),
        compiler_params=params(),
        cost_estimate=pl.CostEstimate(
            flops=4 * number * CAP * count * width,
            bytes_accessed=4 * (count + number * CAP) * width,
            transcendentals=0,
        ),
        name="fill",
    )(ids, routes, gates, tokens, cotangent)
    return out[:number], out[number : 2 * number], out[2 * number :]


def unit_values(x, w, gate_ref, up_ref, down_ref):
    pre_gate = dot_nn(x, gate_ref[...])
    pre_up = dot_nn(x, up_ref[...])
    grad_hidden = dot_nn(w, down_ref[...])
    sig = jax.nn.sigmoid(pre_gate)
    act = pre_gate * sig
    grad_gate = grad_hidden * pre_up * sig * (1.0 + pre_gate * (1.0 - sig))
    return (act * pre_up).astype(BF16), grad_gate.astype(BF16), (grad_hidden * act).astype(BF16)


def store_planes(out_ref, values):
    for k, value in enumerate(values):
        out_ref[k] = value


def first_units(routes, gates, tokens, cotangent, mats, tiles):
    count, width = tokens.shape
    units = mats[0].shape[1] // 2
    number = len(tiles)
    tn = tile_of(units, 256, 128)

    def body(route_ref, gates_ref, tok_ref, cot_ref, gate_ref, up_ref, down_ref, *refs):
        out_ref = refs[0]
        x_refs, w_refs = refs[1 : 1 + number], refs[1 + number : 1 + 2 * number]
        pick_refs, gate_col = refs[1 + 2 * number : 1 + 3 * number], refs[1 + 3 * number]

        @pl.when(pl.program_id(0) == 0)
        def _():
            me = lax.axis_index("expert")
            route_tiles(me, route_ref, gates_ref, pick_refs, gate_col, tiles)
            fill_rows(pick_refs, gate_col, tok_ref, cot_ref, x_refs, w_refs)

        values = unit_values(x_refs[0][...], w_refs[0][...], gate_ref, up_ref, down_ref)
        store_planes(out_ref, values)

    once = lambda shape: pl.BlockSpec(
        shape, lambda j: (0, 0), pipeline_mode=pl.Buffered(1)
    )
    whole = lambda shape: pl.BlockSpec(shape, lambda j: (0, 0))
    out = pl.pallas_call(
        body,
        out_shape=[jax.ShapeDtypeStruct((3, CAP, units), BF16)]
        + [jax.ShapeDtypeStruct((CAP, width), BF16)] * (2 * number)
        + [jax.ShapeDtypeStruct((CAP, count), BF16)] * number,
        grid_spec=pl.GridSpec(
            grid=(units // tn,),
            in_specs=[once((2, count)), once((2, count)), once((count, width)), once((count, width))]
            + [pl.BlockSpec((width, tn), lambda j: (0, j))] * 3,
            out_specs=[pl.BlockSpec((3, CAP, tn), lambda j: (0, 0, j))]
            + [whole((CAP, width))] * (2 * number)
            + [whole((CAP, count))] * number,
            scratch_shapes=[pltpu.VMEM((number * CAP, 128), F32)],
        ),
        compiler_params=params(),
        cost_estimate=pl.CostEstimate(
            flops=6 * CAP * width * units,
            bytes_accessed=2 * (3 * width * units + 2 * (count + number * CAP) * width),
            transcendentals=CAP * units,
        ),
        name="first",
    )(routes, gates, tokens, cotangent, *mats)
    return out[0], out[1 : 1 + number], out[1 + number : 1 + 2 * number], out[1 + 2 * number :]


def expert_units(x_tiles, w_tiles, mats, after, second_half=False):
    number = len(x_tiles)
    slots = number * CAP
    width, units = mats[0].shape
    half = units // 2
    tn = tile_of(half, 256, 128) if second_half else half
    skip = half // tn if second_half else 0
    outs = 1 if second_half else 2

    def body(*refs):
        x, w = stacked(refs[:number]), stacked(refs[number : 2 * number])
        gate_ref, up_ref, down_ref = refs[2 * number : 2 * number + 3]
        values = unit_values(x, w, gate_ref, up_ref, down_ref)
        if second_half:
            store_planes(refs[-1], values)
        else:
            for k in range(2):
                pl.when(pl.program_id(0) == k)(
                    functools.partial(store_planes, refs[k - 2], values)
                )

    tile = pl.BlockSpec((CAP, width), lambda j: (0, 0), pipeline_mode=pl.Buffered(1))
    mat = pl.BlockSpec((width, tn), lambda j: (0, skip + j))
    column = (lambda j: (0, 0, j)) if second_half else (lambda j: (0, 0, 0))
    return pl.pallas_call(
        body,
        out_shape=[jax.ShapeDtypeStruct((3, slots, half), BF16)] * outs,
        grid=(half // tn if second_half else 2,),
        in_specs=[tile] * (2 * number) + [mat] * 3 + [free] * len(after),
        out_specs=[pl.BlockSpec((3, slots, tn), column)] * outs,
        compiler_params=params(),
        cost_estimate=pl.CostEstimate(
            flops=3 * outs * slots * width * units,
            bytes_accessed=outs * (3 * width * units + 2 * slots * width + 3 * slots * units),
            transcendentals=slots * units,
        ),
        name="units",
    )(*x_tiles, *w_tiles, *mats, *after)


def row_gradients(parts, gate_matrix, up_matrix):
    splits = [len(part) for part in parts]
    values = flat(parts)
    number = len(values)
    slots = sum(part[0].shape[1] for part in parts)
    tiles = slots // CAP
    width, units = gate_matrix.shape
    tn = tile_of(width, 768, 128)

    def body(*refs):
        value_refs, (gate_ref, up_ref) = refs[:number], refs[number : number + 2]
        outs = refs[number + 2 :]
        grads = dot_nt(planes(value_refs, splits, 1), gate_ref[...])
        grads = grads + dot_nt(planes(value_refs, splits, 2), up_ref[...])
        grads = grads.astype(BF16)
        for r in range(tiles):
            outs[r][...] = grads[r * CAP : (r + 1) * CAP]

    mat = pl.BlockSpec((tn, units), lambda j: (j, 0))
    return pl.pallas_call(
        body,
        out_shape=[jax.ShapeDtypeStruct((CAP, width), BF16)] * tiles,
        grid=(width // tn,),
        in_specs=held(values) + [mat] * 2,
        out_specs=[pl.BlockSpec((CAP, tn), lambda j: (0, j))] * tiles,
        compiler_params=params(),
        cost_estimate=pl.CostEstimate(
            flops=4 * slots * width * units,
            bytes_accessed=2 * (2 * width * units + slots * width + 3 * slots * units),
            transcendentals=0,
        ),
        name="rows",
    )(*values, gate_matrix, up_matrix)


def square_sum(ids, x_tiles, w_tiles, parts, rows, owners):
    number = len(x_tiles)
    width = x_tiles[0].shape[1]
    units = sum(piece.shape[2] for piece in parts[0])
    splits = [len(part) for part in parts]
    values = flat(parts)
    turned = rows % 128 == 0
    tm = rows if turned else tile_of(width, 384, 128)
    slots = number * CAP

    def body(ids_ref, *refs):
        x, w = stacked(refs[:number]), stacked(refs[number : 2 * number])
        value_refs = refs[2 * number : 2 * number + len(values)]
        out_ref, *own_refs, acc = refs[2 * number + len(values) :]

        @pl.when(pl.program_id(0) == 0)
        def _():
            acc[...] = jnp.zeros_like(acc)

        if turned:

            for k, owner in enumerate(owners):

                @pl.when(pl.program_id(0) == owner(ids_ref[0]))
                def _(k=k):
                    own_refs[2 * k][...] = x.T
                    own_refs[2 * k + 1][...] = w.T

        total = acc[...]
        for k, left in enumerate((w, x, x)):
            grads = dot_tn(left, planes(value_refs, splits, k)).astype(BF16).astype(F32)
            total = total + jnp.sum((grads * grads).reshape(tm // 8, 8, units), axis=0)
        acc[...] = total

        @pl.when(pl.program_id(0) == pl.num_programs(0) - 1)
        def _():
            out_ref[...] = jnp.full((8, 128), jnp.sum(acc[...]), F32)

    tile = pl.BlockSpec((CAP, tm), lambda j, ids: (0, j))
    out = pl.pallas_call(
        body,
        out_shape=[jax.ShapeDtypeStruct((8, 128), F32)]
        + [jax.ShapeDtypeStruct((rows, slots), BF16)] * (2 * len(owners) * turned),
        grid_spec=pltpu.PrefetchScalarGridSpec(
            num_scalar_prefetch=1,
            grid=(width // tm,),
            in_specs=[tile] * (2 * number) + held(values),
            out_specs=[pl.BlockSpec((8, 128), lambda j, ids: (0, 0))]
            + [pl.BlockSpec((rows, slots), lambda j, ids: (0, 0))] * (2 * len(owners) * turned),
            scratch_shapes=[pltpu.VMEM((8, units), F32)],
        ),
        compiler_params=params(),
        cost_estimate=pl.CostEstimate(
            flops=6 * slots * width * units,
            bytes_accessed=2 * (2 * slots * width + 3 * slots * units),
            transcendentals=0,
        ),
        name="squares",
    )(ids, *x_tiles, *w_tiles, *values)
    if turned:
        return out

    def rows_of(tiles, index):
        mine = [lax.dynamic_slice_in_dim(tile, index * rows, rows, 1) for tile in tiles]
        return jnp.concatenate(mine, axis=0)

    result = [out[0]]
    for owner in owners:
        index = owner(ids[0])
        result += own_columns(rows_of(x_tiles, index), rows_of(w_tiles, index))
    return result


def own_columns(x_own, w_own):
    slots, rows = x_own.shape

    def body(x_ref, w_ref, xt_ref, wt_ref):
        xt_ref[...] = x_ref[...].T
        wt_ref[...] = w_ref[...].T

    return pl.pallas_call(
        body,
        out_shape=[jax.ShapeDtypeStruct((rows, slots), BF16)] * 2,
        compiler_params=pltpu.CompilerParams(vmem_limit_bytes=VMEM),
        name="own",
    )(x_own, w_own)


def gradient_rows(x_ref, w_ref, refs):
    x, w = x_ref[...], w_ref[...]
    for k, left in enumerate((w, x, x)):
        value = jnp.concatenate([ref[k] for ref in refs], axis=0)
        yield (k + 2) % 3, dot_nn(left, value).astype(BF16)


def rows_cost(halves, slots, rows, units):
    return pl.CostEstimate(
        flops=3 * halves * slots * rows * units,
        bytes_accessed=halves * (2 * slots * rows + 3 * (slots + rows) * units),
        transcendentals=0,
    )


def clipped_rows(ids, scale, x_own, w_own, groups, out, owner, shards, only=None):
    rows, slots = x_own.shape
    half = groups[0][0].shape[2]
    number = len(groups[0])
    halves = len(groups)
    operands = [ids, scale, x_own, w_own, *flat(groups)]
    specs = [pl.BlockSpec(memory_space=pltpu.SMEM)]
    specs += [pl.BlockSpec((rows, slots), lambda j, ids: (0, 0))] * 2 + held(flat(groups))

    def body(ids_ref, scale_ref, x_ref, w_ref, *rest):
        for h in range(halves):
            part = rest[h * number : (h + 1) * number]
            for k, grads in gradient_rows(x_ref, w_ref, part):
                clipped = (grads.astype(F32) * scale_ref[0, 0]).astype(BF16)
                rest[-1][k, :, h * half : (h + 1) * half] = clipped

    if only is None:
        column = lambda j, ids: (0, 0, owner(ids[0]))
    else:
        column = lambda j, ids: (0, 0, owner(ids[0]) * 2 + only)
    aliases = {}
    if out is not None:
        aliases = {len(operands): 0}
        operands.append(out)
        specs.append(free)
    return pl.pallas_call(
        body,
        out_shape=jax.ShapeDtypeStruct((3, rows, 2 * half * shards), BF16),
        grid_spec=pltpu.PrefetchScalarGridSpec(
            num_scalar_prefetch=1,
            grid=(1,),
            in_specs=specs,
            out_specs=pl.BlockSpec((3, rows, halves * half), column),
        ),
        input_output_aliases=aliases,
        compiler_params=params(),
        cost_estimate=rows_cost(halves, slots, rows, 2 * half),
        name="clip",
    )(*operands)


def given_rows(x_other, w_other, group):
    rows, slots = x_other.shape
    half = group[0].shape[2]
    tn = tile_of(half, 256, 128)

    def body(x_ref, w_ref, *rest):
        for k, grads in gradient_rows(x_ref, w_ref, rest[:-1]):
            rest[-1][k] = grads

    block = lambda size: pl.BlockSpec((3, size, tn), lambda j: (0, 0, j))
    return pl.pallas_call(
        body,
        out_shape=jax.ShapeDtypeStruct((3, rows, half), BF16),
        grid=(half // tn,),
        in_specs=[pl.BlockSpec((rows, slots), lambda j: (0, 0))] * 2
        + [block(piece.shape[1]) for piece in group],
        out_specs=block(rows),
        compiler_params=params(),
        cost_estimate=rows_cost(1, slots, rows, 2 * half),
        name="give",
    )(x_other, w_other, *group)


def placed_rows(ids, scale, first, second, out, owners, tokens=None):
    _, rows, half = first.shape
    block = pl.BlockSpec((3, rows, half), lambda j, ids: (0, 0, 0))
    operands = [ids, scale, first, second]
    specs = [pl.BlockSpec(memory_space=pltpu.SMEM), block, block]
    out_shape = [jax.ShapeDtypeStruct(out.shape, BF16)]

    def column(j, ids):
        return (0, 0, jnp.where(j == 0, owners[0](ids[0]) * 2, owners[1](ids[0]) * 2 + 1))

    out_specs = [pl.BlockSpec((3, rows, half), column)]
    others = []
    if tokens is not None:
        mine, others = tokens
        count = mine.shape[2]
        operands += [mine, *others]
        specs.append(pl.BlockSpec((1, rows, count), lambda j, ids: (ids[0] // 2, 0, 0)))
        specs += [pl.BlockSpec((rows, count), lambda j, ids: (0, 0)) for _ in others]
        out_shape.append(jax.ShapeDtypeStruct((rows, count), BF16))
        out_specs.append(pl.BlockSpec((rows, count), lambda j, ids: (0, 0)))
    aliases = {len(operands): 0}
    operands.append(out)
    specs.append(free)

    def body(ids_ref, scale_ref, first_ref, second_ref, *rest):
        out_ref = rest[-len(out_shape)]
        for j, ref in enumerate((first_ref, second_ref)):

            @pl.when(pl.program_id(0) == j)
            def _(ref=ref):
                out_ref[...] = (ref[...].astype(F32) * scale_ref[0, 0]).astype(BF16)

        if tokens is not None:

            @pl.when(pl.program_id(0) == 0)
            def _():
                total = rest[0][0]
                for part in rest[1 : 1 + len(others)]:
                    total = total + part[...].astype(F32)
                rest[-1][...] = total.astype(BF16)

    return pl.pallas_call(
        body,
        out_shape=out_shape,
        grid_spec=pltpu.PrefetchScalarGridSpec(
            num_scalar_prefetch=1, grid=(2,), in_specs=specs, out_specs=out_specs
        ),
        input_output_aliases=aliases,
        compiler_params=params(),
        cost_estimate=pl.CostEstimate(
            flops=6 * rows * half, bytes_accessed=24 * rows * half, transcendentals=0
        ),
        name="place",
    )(*operands)


def token_sums(tiles, picks):
    number = len(tiles)
    width = tiles[0].shape[1]
    count = picks[0].shape[1]
    tn = tile_of(width, 768, 128)

    def body(*refs):
        rows, pick = stacked(refs[:number]), stacked(refs[number : 2 * number])
        refs[2 * number][...] = dot_tn(rows, pick)

    return pl.pallas_call(
        body,
        out_shape=jax.ShapeDtypeStruct((width, count), F32),
        grid=(width // tn,),
        in_specs=[pl.BlockSpec((CAP, tn), lambda j: (0, j))] * number
        + [pl.BlockSpec((CAP, count), lambda j: (0, 0))] * number,
        out_specs=pl.BlockSpec((tn, count), lambda j: (j, 0)),
        compiler_params=params(),
        cost_estimate=pl.CostEstimate(
            flops=2 * number * CAP * width * count,
            bytes_accessed=2 * number * CAP * width + 4 * width * count,
            transcendentals=0,
        ),
        name="combine",
    )(*tiles, *picks)


def per_device(tokens, cotangent, routes, gate_values, gate_weight, up_weight, down_weight):
    experts = lax.axis_size("expert")
    shards = lax.axis_size("dp")
    width = tokens.shape[1]
    gate_matrix, up_matrix, down_matrix = gate_weight[0], up_weight[0], down_weight[0]
    units = gate_matrix.shape[1]
    half = shards // 2
    rows = width // shards
    ids = jnp.stack([lax.axis_index("dp"), lax.axis_index("expert")]).astype(jnp.int32)

    def swap(value, axis, size, bit):
        return lax.ppermute(value, axis, [(i, i ^ bit) for i in range(size)])

    mats = (gate_matrix, up_matrix, down_matrix)
    near = min(2, experts)
    middle = (near + experts) // 2
    groups = [range(r, r + 1) for r in range(near)]
    groups += [g for g in (range(near, middle), range(middle, experts)) if len(g)]
    inputs = (routes.T, gate_values.T, tokens, cotangent)
    value, x_send, w_send, picks = first_units(*inputs, mats, range(near))
    x_tiles, w_tiles = [x_send[0]], [w_send[0]]
    (other,) = expert_units(x_tiles, w_tiles, mats, [value], second_half=True)
    own = [(value, other)]
    if experts > near:
        more = fill_tiles(ids, *inputs, range(near, experts))
        x_send, w_send, picks = [list(p) + list(q) for p, q in zip((x_send, w_send, picks), more)]
    for r in range(1, experts):
        x_tiles.append(swap(x_send[r], "expert", experts, r))
        w_tiles.append(swap(w_send[r], "expert", experts, r))
    for group in groups[1:]:
        part = slice(group[0], group[-1] + 1)
        own.append(tuple(expert_units(x_tiles[part], w_tiles[part], mats, [own[-1][-1]])))

    order = [2 * i for i in range(half)] + [2 * i + 1 for i in reversed(range(half))]
    right = [(order[p], order[(p + 1) % shards]) for p in range(shards)]
    left = [(b, a) for a, b in right]

    def owner_at(step):
        def owner(index):
            place = jnp.where(index % 2 == 0, index // 2, shards - 1 - index // 2)
            source = (place + shards - step) % shards
            return jnp.where(source < half, 2 * source, 2 * (shards - 1 - source) + 1)

        return owner

    def pass_on(value, way):
        return lax.ppermute(value, "dp", right if way == "r" else left)

    def hop(parts, way, halves=(0, 1)):
        return [{h: pass_on(part[h], way) for h in halves} for part in parts]

    def half_of(parts, h):
        return [part[h] for part in parts]

    total, x_own, w_own, x_right, w_right, x_left, w_left = square_sum(
        ids, x_tiles, w_tiles, own, rows, (owner_at(0), owner_at(-1), owner_at(1))
    )

    chunks = {0: own}
    from_left, from_right = own, own
    for step in range(1, half - 1):
        from_left, from_right = hop(from_left, "r"), hop(from_right, "l")
        chunks[step] = from_left
        chunks[shards - step] = from_right
    give = given_rows(x_right, w_right, half_of(from_left, 1))
    right_b = pass_on(give, "r")
    give = given_rows(x_left, w_left, half_of(from_right, 0))
    left_a = pass_on(give, "l")
    from_left = hop(from_left, "r", (0,))
    from_right = hop(from_right, "l", (1,))
    give = given_rows(x_right, w_right, half_of(from_left, 0))
    right_a = pass_on(give, "r")
    give = given_rows(x_left, w_left, half_of(from_right, 1))
    left_b = pass_on(give, "l")

    bit = 1
    while bit < experts:
        total = total + swap(total, "expert", experts, bit)
        bit *= 2
    shares = [total]
    for k in range(1, shards):
        shares.append(swap(total, "dp", shards, k))
    total = functools.reduce(lambda a, b: a + b, shares)
    clip_limit = CLIP_RMS * math.sqrt(3.0 * experts * width * units * shards)
    scale = clip_limit / jnp.maximum(jnp.sqrt(total[0:1, 0:1]), clip_limit)

    sent = []
    for part in [own[:near]] + [[part] for part in own[near:]]:
        sent += row_gradients(part, gate_matrix, up_matrix)
    back = sent[:1]
    for r in range(1, experts):
        back.append(swap(sent[r], "expert", experts, r))
    outer, inner = ids[0] // 2, ids[0] % 2
    partial = token_sums(back, picks).reshape(half, 2, rows, tokens.shape[0])
    send = lax.dynamic_index_in_dim(partial, 1 - inner, 1, keepdims=False).astype(BF16)
    keep = lax.dynamic_index_in_dim(partial, inner, 1, keepdims=False)
    other = swap(send, "dp", shards, 1)
    sums = keep + other.astype(F32)
    parts = []
    for turn in range(1, half):
        part = lax.dynamic_index_in_dim(sums, (outer + turn) % half, 0, keepdims=False).astype(BF16)
        route = [(2 * i + j, 2 * ((i + turn) % half) + j) for i in range(half) for j in range(2)]
        parts.append(lax.ppermute(part, "dp", route))
    common = (ids, scale, x_own, w_own)
    out = None
    for step in clip_order(shards):
        groups = [half_of(chunks[step], h) for h in range(2)]
        out = clipped_rows(*common, groups, out, owner_at(step), shards)
    for h, step, parts_at in ((0, half - 1, from_left), (1, half + 1, from_right)):
        group = [half_of(parts_at, h)]
        out = clipped_rows(*common, group, out, owner_at(step), shards, only=h)
    owners = (owner_at(half + 1), owner_at(half - 1))
    (out,) = placed_rows(ids, scale, left_a, right_b, out, owners)
    owners = (owner_at(half), owner_at(half))
    out, d_tokens = placed_rows(ids, scale, right_a, left_b, out, owners, (sums, parts))
    return (out[None], d_tokens)


def clip_order(shards):
    return [0] + [s for step in range(1, shards // 2 - 1) for s in (step, shards - step)]


def solution(mesh):
    return jax.shard_map(
        per_device,
        mesh=mesh,
        in_specs=(
            P("expert", None),
            P("expert", None),
            P("expert", None),
            P("expert", None),
            P("expert", None, "dp"),
            P("expert", None, "dp"),
            P("expert", None, "dp"),
        ),
        out_specs=(P("expert", None, "dp", None), P("dp", "expert")),
        check_vma=False,
    )
```

```python
import functools
import math

import jax
import jax.numpy as jnp
from jax import lax
from jax.experimental import pallas as pl
from jax.experimental.pallas import tpu as pltpu
from jax.sharding import PartitionSpec as P


CAP = 128
CLIP_RMS = 0.2
VMEM = 67043328


F32 = jnp.float32
BF16 = jnp.bfloat16


def tile_of(size, largest, unit):
    best = size
    for tile in range(unit, min(size, largest) + 1, unit):
        if size % tile == 0:
            best = tile
    return best


def params(dims=1):
    return pltpu.CompilerParams(
        dimension_semantics=("arbitrary",) * dims, vmem_limit_bytes=VMEM
    )


def dot_nn(left, right):
    return lax.dot_general(left, right, (((1,), (0,)), ((), ())), preferred_element_type=F32)


def dot_nt(left, right):
    return lax.dot_general(left, right, (((1,), (1,)), ((), ())), preferred_element_type=F32)


def dot_tn(left, right):
    return lax.dot_general(left, right, (((0,), (0,)), ((), ())), preferred_element_type=F32)


free = pl.BlockSpec(memory_space=pl.ANY)


def planes(refs, splits, plane):
    tiles, at = [], 0
    for count in splits:
        pieces = [ref[plane] for ref in refs[at : at + count]]
        tiles.append(pieces[0] if count == 1 else jnp.concatenate(pieces, axis=1))
        at += count
    return tiles[0] if len(tiles) == 1 else jnp.concatenate(tiles, axis=0)


def flat(parts):
    return [piece for part in parts for piece in part]


def held(values):
    return [pl.BlockSpec(value.shape, lambda *_: (0, 0, 0)) for value in values]


def stacked(refs):
    tiles = [ref[...] for ref in refs]
    return tiles[0] if len(tiles) == 1 else jnp.concatenate(tiles, axis=0)


def route_tiles(me, route_ref, gate_ref, pick_refs, gate_col, tiles):
    count = route_ref.shape[1]
    first, second = route_ref[0:1, :], route_ref[1:2, :]
    gates = gate_ref[...].astype(F32)
    hits = [jnp.logical_or(first == (me ^ r), second == (me ^ r)).astype(F32) for r in tiles]
    pad = (-len(tiles)) % 8
    rows = jnp.concatenate(hits + [jnp.zeros((pad, count), F32)] * (pad > 0), axis=0)
    earlier = (
        lax.broadcasted_iota(jnp.int32, (count, count), 0)
        < lax.broadcasted_iota(jnp.int32, (count, count), 1)
    ).astype(F32)
    before = dot_nn(rows.astype(BF16), earlier.astype(BF16))
    slot = lax.broadcasted_iota(jnp.int32, (CAP, count), 0).astype(F32)
    for k, r in enumerate(tiles):
        match = jnp.logical_and(slot == before[k : k + 1, :], hits[k] > 0.5)
        pick = jnp.where(match, 1.0, 0.0)
        weight = jnp.where(first == (me ^ r), gates[0:1, :], gates[1:2, :])
        gate_col[k * CAP : (k + 1) * CAP, :] = jnp.broadcast_to(
            jnp.sum(pick * weight, axis=1, keepdims=True), (CAP, 128)
        )
        pick_refs[k][...] = pick.astype(BF16)


def fill_rows(pick_refs, gate_col, tok_ref, cot_ref, x_refs, w_refs):
    pick = stacked(pick_refs)
    rows = dot_nn(pick, tok_ref[...])
    scaled = dot_nn(pick, cot_ref[...]) * gate_col[:, 0:1]
    for k in range(len(x_refs)):
        part = slice(k * CAP, (k + 1) * CAP)
        x_refs[k][...] = rows[part].astype(BF16)
        w_refs[k][...] = scaled[part].astype(BF16)


def fill_tiles(ids, routes, gates, tokens, cotangent, tiles):
    count, width = tokens.shape
    number = len(tiles)
    tn = tile_of(width, 1536, 128)

    def body(ids_ref, route_ref, gate_ref, tok_ref, cot_ref, *refs):
        x_refs, w_refs = refs[:number], refs[number : 2 * number]
        pick_refs, gate_col = refs[2 * number : 3 * number], refs[3 * number]

        @pl.when(pl.program_id(0) == 0)
        def _():
            route_tiles(ids_ref[1], route_ref, gate_ref, pick_refs, gate_col, tiles)

        fill_rows(pick_refs, gate_col, tok_ref, cot_ref, x_refs, w_refs)

    whole = lambda shape: pl.BlockSpec(shape, lambda j, ids: (0, 0))
    cols = lambda rows: pl.BlockSpec((rows, tn), lambda j, ids: (0, j))
    out = pl.pallas_call(
        body,
        out_shape=[jax.ShapeDtypeStruct((CAP, width), BF16)] * (2 * number)
        + [jax.ShapeDtypeStruct((CAP, count), BF16)] * number,
        grid_spec=pltpu.PrefetchScalarGridSpec(
            num_scalar_prefetch=1,
            grid=(width // tn,),
            in_specs=[whole((2, count)), whole((2, count)), cols(count), cols(count)],
            out_specs=[cols(CAP)] * (2 * number) + [whole((CAP, count))] * number,
            scratch_shapes=[pltpu.VMEM((number * CAP, 128), F32)],
        ),
        compiler_params=params(),
        cost_estimate=pl.CostEstimate(
            flops=4 * number * CAP * count * width,
            bytes_accessed=4 * (count + number * CAP) * width,
            transcendentals=0,
        ),
        name="fill",
    )(ids, routes, gates, tokens, cotangent)
    return out[:number], out[number : 2 * number], out[2 * number :]


def unit_values(x, w, gate_ref, up_ref, down_ref):
    pre_gate = dot_nn(x, gate_ref[...])
    pre_up = dot_nn(x, up_ref[...])
    grad_hidden = dot_nn(w, down_ref[...])
    sig = jax.nn.sigmoid(pre_gate)
    act = pre_gate * sig
    grad_gate = grad_hidden * pre_up * sig * (1.0 + pre_gate * (1.0 - sig))
    return (act * pre_up).astype(BF16), grad_gate.astype(BF16), (grad_hidden * act).astype(BF16)


def store_planes(out_ref, values):
    for k, value in enumerate(values):
        out_ref[k] = value


def first_units(routes, gates, tokens, cotangent, mats, tiles):
    count, width = tokens.shape
    units = mats[0].shape[1] // 2
    number = len(tiles)
    tn = tile_of(units, 256, 128)

    def body(route_ref, gates_ref, tok_ref, cot_ref, gate_ref, up_ref, down_ref, *refs):
        out_ref = refs[0]
        x_refs, w_refs = refs[1 : 1 + number], refs[1 + number : 1 + 2 * number]
        pick_refs, gate_col = refs[1 + 2 * number : 1 + 3 * number], refs[1 + 3 * number]

        @pl.when(pl.program_id(0) == 0)
        def _():
            me = lax.axis_index("expert")
            route_tiles(me, route_ref, gates_ref, pick_refs, gate_col, tiles)
            fill_rows(pick_refs, gate_col, tok_ref, cot_ref, x_refs, w_refs)

        values = unit_values(x_refs[0][...], w_refs[0][...], gate_ref, up_ref, down_ref)
        store_planes(out_ref, values)

    once = lambda shape: pl.BlockSpec(
        shape, lambda j: (0, 0), pipeline_mode=pl.Buffered(1)
    )
    whole = lambda shape: pl.BlockSpec(shape, lambda j: (0, 0))
    out = pl.pallas_call(
        body,
        out_shape=[jax.ShapeDtypeStruct((3, CAP, units), BF16)]
        + [jax.ShapeDtypeStruct((CAP, width), BF16)] * (2 * number)
        + [jax.ShapeDtypeStruct((CAP, count), BF16)] * number,
        grid_spec=pl.GridSpec(
            grid=(units // tn,),
            in_specs=[once((2, count)), once((2, count)), once((count, width)), once((count, width))]
            + [pl.BlockSpec((width, tn), lambda j: (0, j))] * 3,
            out_specs=[pl.BlockSpec((3, CAP, tn), lambda j: (0, 0, j))]
            + [whole((CAP, width))] * (2 * number)
            + [whole((CAP, count))] * number,
            scratch_shapes=[pltpu.VMEM((number * CAP, 128), F32)],
        ),
        compiler_params=params(),
        cost_estimate=pl.CostEstimate(
            flops=6 * CAP * width * units,
            bytes_accessed=2 * (3 * width * units + 2 * (count + number * CAP) * width),
            transcendentals=CAP * units,
        ),
        name="first",
    )(routes, gates, tokens, cotangent, *mats)
    return out[0], out[1 : 1 + number], out[1 + number : 1 + 2 * number], out[1 + 2 * number :]


def expert_units(x_tiles, w_tiles, mats, after, second_half=False):
    number = len(x_tiles)
    slots = number * CAP
    width, units = mats[0].shape
    half = units // 2
    tn = tile_of(half, 256, 128) if second_half else half
    skip = half // tn if second_half else 0
    outs = 1 if second_half else 2

    def body(*refs):
        x, w = stacked(refs[:number]), stacked(refs[number : 2 * number])
        gate_ref, up_ref, down_ref = refs[2 * number : 2 * number + 3]
        values = unit_values(x, w, gate_ref, up_ref, down_ref)
        if second_half:
            store_planes(refs[-1], values)
        else:
            for k in range(2):
                pl.when(pl.program_id(0) == k)(
                    functools.partial(store_planes, refs[k - 2], values)
                )

    tile = pl.BlockSpec((CAP, width), lambda j: (0, 0), pipeline_mode=pl.Buffered(1))
    mat = pl.BlockSpec((width, tn), lambda j: (0, skip + j))
    column = (lambda j: (0, 0, j)) if second_half else (lambda j: (0, 0, 0))
    return pl.pallas_call(
        body,
        out_shape=[jax.ShapeDtypeStruct((3, slots, half), BF16)] * outs,
        grid=(half // tn if second_half else 2,),
        in_specs=[tile] * (2 * number) + [mat] * 3 + [free] * len(after),
        out_specs=[pl.BlockSpec((3, slots, tn), column)] * outs,
        compiler_params=params(),
        cost_estimate=pl.CostEstimate(
            flops=3 * outs * slots * width * units,
            bytes_accessed=outs * (3 * width * units + 2 * slots * width + 3 * slots * units),
            transcendentals=slots * units,
        ),
        name="units",
    )(*x_tiles, *w_tiles, *mats, *after)


def row_gradients(parts, gate_matrix, up_matrix):
    splits = [len(part) for part in parts]
    values = flat(parts)
    number = len(values)
    slots = sum(part[0].shape[1] for part in parts)
    tiles = slots // CAP
    width, units = gate_matrix.shape
    tn = tile_of(width, 768, 128)

    def body(*refs):
        value_refs, (gate_ref, up_ref) = refs[:number], refs[number : number + 2]
        outs = refs[number + 2 :]
        grads = dot_nt(planes(value_refs, splits, 1), gate_ref[...])
        grads = grads + dot_nt(planes(value_refs, splits, 2), up_ref[...])
        grads = grads.astype(BF16)
        for r in range(tiles):
            outs[r][...] = grads[r * CAP : (r + 1) * CAP]

    mat = pl.BlockSpec((tn, units), lambda j: (j, 0))
    return pl.pallas_call(
        body,
        out_shape=[jax.ShapeDtypeStruct((CAP, width), BF16)] * tiles,
        grid=(width // tn,),
        in_specs=held(values) + [mat] * 2,
        out_specs=[pl.BlockSpec((CAP, tn), lambda j: (0, j))] * tiles,
        compiler_params=params(),
        cost_estimate=pl.CostEstimate(
            flops=4 * slots * width * units,
            bytes_accessed=2 * (2 * width * units + slots * width + 3 * slots * units),
            transcendentals=0,
        ),
        name="rows",
    )(*values, gate_matrix, up_matrix)


def square_sum(ids, x_tiles, w_tiles, parts, rows, owners):
    number = len(x_tiles)
    width = x_tiles[0].shape[1]
    units = sum(piece.shape[2] for piece in parts[0])
    splits = [len(part) for part in parts]
    values = flat(parts)
    turned = rows % 128 == 0
    tm = rows if turned else tile_of(width, 384, 128)
    slots = number * CAP

    def body(ids_ref, *refs):
        x, w = stacked(refs[:number]), stacked(refs[number : 2 * number])
        value_refs = refs[2 * number : 2 * number + len(values)]
        out_ref, *own_refs, acc = refs[2 * number + len(values) :]

        @pl.when(pl.program_id(0) == 0)
        def _():
            acc[...] = jnp.zeros_like(acc)

        if turned:

            for k, owner in enumerate(owners):

                @pl.when(pl.program_id(0) == owner(ids_ref[0]))
                def _(k=k):
                    own_refs[2 * k][...] = x.T
                    own_refs[2 * k + 1][...] = w.T

        total = acc[...]
        for k, left in enumerate((w, x, x)):
            grads = dot_tn(left, planes(value_refs, splits, k)).astype(BF16).astype(F32)
            total = total + jnp.sum((grads * grads).reshape(tm // 8, 8, units), axis=0)
        acc[...] = total

        @pl.when(pl.program_id(0) == pl.num_programs(0) - 1)
        def _():
            out_ref[...] = jnp.full((8, 128), jnp.sum(acc[...]), F32)

    tile = pl.BlockSpec((CAP, tm), lambda j, ids: (0, j))
    out = pl.pallas_call(
        body,
        out_shape=[jax.ShapeDtypeStruct((8, 128), F32)]
        + [jax.ShapeDtypeStruct((rows, slots), BF16)] * (2 * len(owners) * turned),
        grid_spec=pltpu.PrefetchScalarGridSpec(
            num_scalar_prefetch=1,
            grid=(width // tm,),
            in_specs=[tile] * (2 * number) + held(values),
            out_specs=[pl.BlockSpec((8, 128), lambda j, ids: (0, 0))]
            + [pl.BlockSpec((rows, slots), lambda j, ids: (0, 0))] * (2 * len(owners) * turned),
            scratch_shapes=[pltpu.VMEM((8, units), F32)],
        ),
        compiler_params=params(),
        cost_estimate=pl.CostEstimate(
            flops=6 * slots * width * units,
            bytes_accessed=2 * (2 * slots * width + 3 * slots * units),
            transcendentals=0,
        ),
        name="squares",
    )(ids, *x_tiles, *w_tiles, *values)
    if turned:
        return out

    def rows_of(tiles, index):
        mine = [lax.dynamic_slice_in_dim(tile, index * rows, rows, 1) for tile in tiles]
        return jnp.concatenate(mine, axis=0)

    result = [out[0]]
    for owner in owners:
        index = owner(ids[0])
        result += own_columns(rows_of(x_tiles, index), rows_of(w_tiles, index))
    return result


def own_columns(x_own, w_own):
    slots, rows = x_own.shape

    def body(x_ref, w_ref, xt_ref, wt_ref):
        xt_ref[...] = x_ref[...].T
        wt_ref[...] = w_ref[...].T

    return pl.pallas_call(
        body,
        out_shape=[jax.ShapeDtypeStruct((rows, slots), BF16)] * 2,
        compiler_params=pltpu.CompilerParams(vmem_limit_bytes=VMEM),
        name="own",
    )(x_own, w_own)


def gradient_rows(x_ref, w_ref, refs):
    x, w = x_ref[...], w_ref[...]
    for k, left in enumerate((w, x, x)):
        value = jnp.concatenate([ref[k] for ref in refs], axis=0)
        yield (k + 2) % 3, dot_nn(left, value).astype(BF16)


def rows_cost(halves, slots, rows, units):
    return pl.CostEstimate(
        flops=3 * halves * slots * rows * units,
        bytes_accessed=halves * (2 * slots * rows + 3 * (slots + rows) * units),
        transcendentals=0,
    )


def clipped_rows(ids, scale, x_own, w_own, groups, out, owner, shards, given=None, at=0):
    rows, slots = x_own.shape
    half = groups[0][0].shape[2]
    number = len(groups[0])
    halves = len(groups)
    operands = [ids, scale, x_own, w_own, *flat(groups)]
    specs = [pl.BlockSpec(memory_space=pltpu.SMEM)]
    specs += [pl.BlockSpec((rows, slots), lambda j, ids: (0, 0))] * 2 + held(flat(groups))
    if given is not None:
        operands.append(given)
        specs += held([given])

    def body(ids_ref, scale_ref, x_ref, w_ref, *rest):
        def store(h, k, grads):
            clipped = (grads.astype(F32) * scale_ref[0, 0]).astype(BF16)
            rest[-1][k, :, h * half : (h + 1) * half] = clipped

        for h in range(halves):
            part = rest[h * number : (h + 1) * number]
            for k, grads in gradient_rows(x_ref, w_ref, part):
                store(at + h, k, grads)
        if given is not None:
            for k in range(3):
                store(1 - at, k, rest[number][k])

    aliases = {}
    if out is not None:
        aliases = {len(operands): 0}
        operands.append(out)
        specs.append(free)
    return pl.pallas_call(
        body,
        out_shape=jax.ShapeDtypeStruct((3, rows, 2 * half * shards), BF16),
        grid_spec=pltpu.PrefetchScalarGridSpec(
            num_scalar_prefetch=1,
            grid=(1,),
            in_specs=specs,
            out_specs=pl.BlockSpec(
                (3, rows, 2 * half), lambda j, ids: (0, 0, owner(ids[0]))
            ),
        ),
        input_output_aliases=aliases,
        compiler_params=params(),
        cost_estimate=rows_cost(halves, slots, rows, 2 * half),
        name="clip",
    )(*operands)


def given_rows(x_other, w_other, group):
    rows, slots = x_other.shape
    half = group[0].shape[2]
    tn = tile_of(half, 256, 128)

    def body(x_ref, w_ref, *rest):
        for k, grads in gradient_rows(x_ref, w_ref, rest[:-1]):
            rest[-1][k] = grads

    block = lambda size: pl.BlockSpec((3, size, tn), lambda j: (0, 0, j))
    return pl.pallas_call(
        body,
        out_shape=jax.ShapeDtypeStruct((3, rows, half), BF16),
        grid=(half // tn,),
        in_specs=[pl.BlockSpec((rows, slots), lambda j: (0, 0))] * 2
        + [block(piece.shape[1]) for piece in group],
        out_specs=block(rows),
        compiler_params=params(),
        cost_estimate=rows_cost(1, slots, rows, 2 * half),
        name="give",
    )(x_other, w_other, *group)


def placed_rows(ids, scale, first, second, out, owners, tokens=None):
    _, rows, half = first.shape
    block = pl.BlockSpec((3, rows, half), lambda j, ids: (0, 0, 0))
    operands = [ids, scale, first, second]
    specs = [pl.BlockSpec(memory_space=pltpu.SMEM), block, block]
    out_shape = [jax.ShapeDtypeStruct(out.shape, BF16)]

    def column(j, ids):
        return (0, 0, jnp.where(j == 0, owners[0](ids[0]) * 2, owners[1](ids[0]) * 2 + 1))

    out_specs = [pl.BlockSpec((3, rows, half), column)]
    others = []
    if tokens is not None:
        mine, others = tokens
        count = mine.shape[2]
        operands += [mine, *others]
        specs.append(pl.BlockSpec((1, rows, count), lambda j, ids: (ids[0] // 2, 0, 0)))
        specs += [pl.BlockSpec((rows, count), lambda j, ids: (0, 0)) for _ in others]
        out_shape.append(jax.ShapeDtypeStruct((rows, count), BF16))
        out_specs.append(pl.BlockSpec((rows, count), lambda j, ids: (0, 0)))
    aliases = {len(operands): 0}
    operands.append(out)
    specs.append(free)

    def body(ids_ref, scale_ref, first_ref, second_ref, *rest):
        out_ref = rest[-len(out_shape)]
        for j, ref in enumerate((first_ref, second_ref)):

            @pl.when(pl.program_id(0) == j)
            def _(ref=ref):
                out_ref[...] = (ref[...].astype(F32) * scale_ref[0, 0]).astype(BF16)

        if tokens is not None:

            @pl.when(pl.program_id(0) == 0)
            def _():
                total = rest[0][0]
                for part in rest[1 : 1 + len(others)]:
                    total = total + part[...].astype(F32)
                rest[-1][...] = total.astype(BF16)

    return pl.pallas_call(
        body,
        out_shape=out_shape,
        grid_spec=pltpu.PrefetchScalarGridSpec(
            num_scalar_prefetch=1, grid=(2,), in_specs=specs, out_specs=out_specs
        ),
        input_output_aliases=aliases,
        compiler_params=params(),
        cost_estimate=pl.CostEstimate(
            flops=6 * rows * half, bytes_accessed=24 * rows * half, transcendentals=0
        ),
        name="place",
    )(*operands)


def token_sums(ids, tiles, picks, shards):
    number = len(tiles)
    width = tiles[0].shape[1]
    count = picks[0].shape[1]
    rows = width // shards
    half = shards // 2
    cost = pl.CostEstimate(
        flops=2 * number * CAP * width * count,
        bytes_accessed=2 * number * CAP * width + 3 * width * count,
        transcendentals=0,
    )
    if rows % 128:
        tn = tile_of(width, 768, 128)

        def whole(*refs):
            rows_in, pick = stacked(refs[:number]), stacked(refs[number : 2 * number])
            refs[2 * number][...] = dot_tn(rows_in, pick)

        partial = pl.pallas_call(
            whole,
            out_shape=jax.ShapeDtypeStruct((width, count), F32),
            grid=(width // tn,),
            in_specs=[pl.BlockSpec((CAP, tn), lambda j: (0, j))] * number
            + [pl.BlockSpec((CAP, count), lambda j: (0, 0))] * number,
            out_specs=pl.BlockSpec((tn, count), lambda j: (j, 0)),
            compiler_params=params(),
            cost_estimate=cost,
            name="combine",
        )(*tiles, *picks).reshape(half, 2, rows, count)
        inner = ids[0] % 2
        keep = lax.dynamic_index_in_dim(partial, inner, 1, keepdims=False)
        send = lax.dynamic_index_in_dim(partial, 1 - inner, 1, keepdims=False)
        return keep, send.astype(BF16)

    def body(ids_ref, *refs):
        mine, other = stacked(refs[:number]), stacked(refs[number : 2 * number])
        pick = stacked(refs[2 * number : 3 * number])
        keep_ref, send_ref = refs[3 * number :]
        keep_ref[0] = dot_tn(mine, pick)
        send_ref[0] = dot_tn(other, pick).astype(BF16)

    mine = pl.BlockSpec((CAP, rows), lambda j, ids: (0, 2 * j + ids[0] % 2))
    other = pl.BlockSpec((CAP, rows), lambda j, ids: (0, 2 * j + 1 - ids[0] % 2))
    pick = pl.BlockSpec((CAP, count), lambda j, ids: (0, 0))
    block = pl.BlockSpec((1, rows, count), lambda j, ids: (j, 0, 0))
    return pl.pallas_call(
        body,
        out_shape=[
            jax.ShapeDtypeStruct((half, rows, count), F32),
            jax.ShapeDtypeStruct((half, rows, count), BF16),
        ],
        grid_spec=pltpu.PrefetchScalarGridSpec(
            num_scalar_prefetch=1,
            grid=(half,),
            in_specs=[mine] * number + [other] * number + [pick] * number,
            out_specs=[block, block],
        ),
        compiler_params=params(),
        cost_estimate=cost,
        name="combine",
    )(ids, *tiles, *tiles, *picks)


def per_device(tokens, cotangent, routes, gate_values, gate_weight, up_weight, down_weight):
    experts = lax.axis_size("expert")
    shards = lax.axis_size("dp")
    width = tokens.shape[1]
    gate_matrix, up_matrix, down_matrix = gate_weight[0], up_weight[0], down_weight[0]
    units = gate_matrix.shape[1]
    half = shards // 2
    rows = width // shards
    ids = jnp.stack([lax.axis_index("dp"), lax.axis_index("expert")]).astype(jnp.int32)

    def swap(value, axis, size, bit):
        return lax.ppermute(value, axis, [(i, i ^ bit) for i in range(size)])

    mats = (gate_matrix, up_matrix, down_matrix)
    near = min(2, experts)
    middle = (near + experts) // 2
    groups = [range(r, r + 1) for r in range(near)]
    groups += [g for g in (range(near, middle), range(middle, experts)) if len(g)]
    inputs = (routes.T, gate_values.T, tokens, cotangent)
    value, x_send, w_send, picks = first_units(*inputs, mats, range(near))
    x_tiles, w_tiles = [x_send[0]], [w_send[0]]
    (other,) = expert_units(x_tiles, w_tiles, mats, [value], second_half=True)
    own = [(value, other)]
    if experts > near:
        more = fill_tiles(ids, *inputs, range(near, experts))
        x_send, w_send, picks = [list(p) + list(q) for p, q in zip((x_send, w_send, picks), more)]
    for r in range(1, experts):
        x_tiles.append(swap(x_send[r], "expert", experts, r))
        w_tiles.append(swap(w_send[r], "expert", experts, r))
    for group in groups[1:]:
        part = slice(group[0], group[-1] + 1)
        own.append(tuple(expert_units(x_tiles[part], w_tiles[part], mats, [own[-1][-1]])))

    order = [2 * i for i in range(half)] + [2 * i + 1 for i in reversed(range(half))]
    right = [(order[p], order[(p + 1) % shards]) for p in range(shards)]
    left = [(b, a) for a, b in right]

    def owner_at(step):
        def owner(index):
            place = jnp.where(index % 2 == 0, index // 2, shards - 1 - index // 2)
            source = (place + shards - step) % shards
            return jnp.where(source < half, 2 * source, 2 * (shards - 1 - source) + 1)

        return owner

    def pass_on(value, way):
        return lax.ppermute(value, "dp", right if way == "r" else left)

    def hop(parts, way, halves=(0, 1)):
        return [{h: pass_on(part[h], way) for h in halves} for part in parts]

    def half_of(parts, h):
        return [part[h] for part in parts]

    total, x_own, w_own, x_right, w_right, x_left, w_left = square_sum(
        ids, x_tiles, w_tiles, own, rows, (owner_at(0), owner_at(-1), owner_at(1))
    )

    chunks = {0: own}
    from_left, from_right = own, own
    for step in range(1, half - 1):
        from_left, from_right = hop(from_left, "r"), hop(from_right, "l")
        chunks[step] = from_left
        chunks[shards - step] = from_right
    give = given_rows(x_right, w_right, half_of(from_left, 1))
    right_b = pass_on(give, "r")
    give = given_rows(x_left, w_left, half_of(from_right, 0))
    left_a = pass_on(give, "l")
    from_left = hop(from_left, "r", (0,))
    from_right = hop(from_right, "l", (1,))
    give = given_rows(x_right, w_right, half_of(from_left, 0))
    right_a = pass_on(give, "r")
    give = given_rows(x_left, w_left, half_of(from_right, 1))
    left_b = pass_on(give, "l")

    bit = 1
    while bit < experts:
        total = total + swap(total, "expert", experts, bit)
        bit *= 2
    shares = [total]
    for k in range(1, shards):
        shares.append(swap(total, "dp", shards, k))
    total = functools.reduce(lambda a, b: a + b, shares)
    clip_limit = CLIP_RMS * math.sqrt(3.0 * experts * width * units * shards)
    scale = clip_limit / jnp.maximum(jnp.sqrt(total[0:1, 0:1]), clip_limit)

    sent = []
    for part in [own[:near]] + [[part] for part in own[near:]]:
        sent += row_gradients(part, gate_matrix, up_matrix)
    back = sent[:1]
    for r in range(1, experts):
        back.append(swap(sent[r], "expert", experts, r))
    outer = ids[0] // 2
    keep, send = token_sums(ids, back, picks, shards)
    other = swap(send, "dp", shards, 1)
    sums = keep + other.astype(F32)
    parts = []
    for turn in range(1, half):
        part = lax.dynamic_index_in_dim(sums, (outer + turn) % half, 0, keepdims=False).astype(BF16)
        route = [(2 * i + j, 2 * ((i + turn) % half) + j) for i in range(half) for j in range(2)]
        parts.append(lax.ppermute(part, "dp", route))
    common = (ids, scale, x_own, w_own)
    out = None
    for step in clip_order(shards):
        groups = [half_of(chunks[step], h) for h in range(2)]
        out = clipped_rows(*common, groups, out, owner_at(step), shards)
    sides = ((0, half - 1, from_left, right_b), (1, half + 1, from_right, left_a))
    for h, step, parts_at, given in sides:
        group = [half_of(parts_at, h)]
        out = clipped_rows(*common, group, out, owner_at(step), shards, given, h)
    owners = (owner_at(half), owner_at(half))
    out, d_tokens = placed_rows(ids, scale, right_a, left_b, out, owners, (sums, parts))
    return (out[None], d_tokens)


def clip_order(shards):
    return [0] + [s for step in range(1, shards // 2 - 1) for s in (step, shards - step)]


def solution(mesh):
    return jax.shard_map(
        per_device,
        mesh=mesh,
        in_specs=(
            P("expert", None),
            P("expert", None),
            P("expert", None),
            P("expert", None),
            P("expert", None, "dp"),
            P("expert", None, "dp"),
            P("expert", None, "dp"),
        ),
        out_specs=(P("expert", None, "dp", None), P("dp", "expert")),
        check_vma=False,
    )
```
